1024 devices in a mesh: scen: 32 (over z_lo, x), row: 32 (over y, z_hi, core).
Axes of the slice: x: 4, y: 4, z: 32 (z_hi: 4, z_lo: 8; z = z_hi * 8 + z_lo), core: 2. Of those that a mesh axis runs over, the one named last changes fastest.
Arguments:
- border: bfloat16 [512, 8192, 128], P('scen', 'row'), may hold values from -0.119628906 to 0.119628906
- col_index: int32 [512, 128], P('scen'), may hold values from 0 to 4095
- barrier: float32 [4096], replicated, may hold values from 0.3 to 3
- counts: int32 [32], replicated, may hold values from 1 to 16, as said below
- inverse: bfloat16 [1024, 1024], replicated, may hold values from -0.140625 to 0.140625
- slab: float32 [8192, 4096], P('row', 'scen'), may hold values from -1.5 to 1.5
Outputs:
- updated: float32 [8192, 4096], P('row', 'scen')
The draws below stay inside these ranges and needn't reach their ends.
Inputs may be any that keep to these rules, and one draw needn't show every extreme that they name: `counts`: the scenario groups whose index differs by a multiple of 4 from one drawn index hold 16 live blocks; every other group holds 1 to 4.
All inputs are finite; a program needn't handle non-finite values.
Results may differ from the reference program's by a relative error of at most 0.0064.
Values may be sent and summed in bfloat16 or wider, within the bound.
A program may use at most 32 MiB of HBM per device.

```python
import math
import jax
import jax.numpy as jnp
from jax import lax

NF = 8192
PW = 1024
NT = 4096
BW = 128
NCOL = 4096
SLOTS = 16
BLOCKS = 512
N_SCEN = 32
N_ROW = 32


def draw_counts(key, part):
    first_key, second_key = jax.random.split(jax.random.fold_in(key, 11))
    shift_value = jax.random.randint(first_key, (), 0, N_SCEN, dtype=jnp.int32)
    group_ids = jnp.arange(N_SCEN, dtype=jnp.int32)
    light_counts = jax.random.randint(second_key, (N_SCEN,), 1, SLOTS // 4 + 1, dtype=jnp.int32)
    crowded = (group_ids - shift_value) % 4 == 0
    return jnp.where(crowded, SLOTS, light_counts).astype(jnp.int32)


def place_ends(values, stream_key, smallest, largest):
    shape = values.shape
    place = [jax.random.randint(jax.random.fold_in(stream_key, axis), (), 0, shape[axis]) for axis in range(len(shape))]
    values = values.at[tuple(place)].set(smallest)
    longest = shape.index(max(shape))
    place[longest] = (place[longest] + 1) % shape[longest]
    return values.at[tuple(place)].set(largest)


def block_scale(key, dims, cuts, low, high):
    gain, own = 1.0, jax.random.fold_in(key, 6)
    for position, parts in cuts:
        steps = jnp.exp(jax.random.uniform(jax.random.fold_in(own, position), (parts,), jnp.float32, low / len(cuts), high / len(cuts)))
        gain = gain * jnp.repeat(steps, dims[position] // parts).reshape([-1 if axis == position else 1 for axis in range(len(dims))])
    return gain


def scatter_about(stream_key, extent, width, bound, cuts=(), kind=jnp.bfloat16):
    level = block_scale(stream_key, extent, cuts, -0.22, 0.18) if cuts else 1.0
    entries = jax.random.normal(stream_key, extent, jnp.float32) * width * level
    return jnp.minimum(jnp.maximum(entries, -bound), bound).astype(kind)


def setup_inputs(seed: int = 0) -> dict:
    streams_of = jax.random.split(jax.random.key(seed), 7)
    return {
        "border": scatter_about(streams_of[0], (BLOCKS, NF, BW), 0.02, 0.119628906, ((0, 32), (1, 32))),
        "col_index": place_ends(jax.random.randint(streams_of[1], (BLOCKS, BW), 0, NCOL), jax.random.fold_in(streams_of[1], 1), 0, NCOL - 1).astype(jnp.int32),
        "barrier": jnp.clip(jnp.exp(jax.random.uniform(streams_of[2], (NCOL,), jnp.float32, math.log(0.3), math.log(3.0))), 0.3, 3.0),
        "counts": draw_counts(jax.random.fold_in(streams_of[6], 71), 0),
        "inverse": scatter_about(streams_of[4], (PW, PW), (24.0 / PW), 0.140625),
        "slab": scatter_about(streams_of[5], (NF, NT), 0.25, 1.5, ((0, 32), (1, 32)), jnp.float32),
    }


def reference(border, col_index, barrier, counts, inverse, slab):
    share_width = PW // N_ROW
    local_rows = NF // N_ROW
    columns = jnp.arange(PW, dtype=jnp.int32)
    panel_vars = ((columns // share_width) * local_rows + columns % share_width).astype(jnp.int32)
    block_ids = jnp.arange(N_SCEN * SLOTS, dtype=jnp.int32)

    def accumulate(total, number):
        group = number // SLOTS
        within = number % SLOTS
        is_live = within < counts[group]

        def add_block(running):
            block = lax.dynamic_index_in_dim(border, number, 0, keepdims=False)
            indices = lax.dynamic_index_in_dim(col_index, number, 0, keepdims=False)
            weights = barrier[indices]
            scaled = (block.astype(jnp.float32) * weights[None, :]).astype(jnp.bfloat16)
            heads = scaled[panel_vars]
            return running + jnp.dot(scaled, heads.T, preferred_element_type=jnp.float32)

        def keep_block(running):
            return running

        return lax.cond(is_live, add_block, keep_block, total), None

    panel, unused = lax.scan(accumulate, jnp.zeros((NF, PW), jnp.float32), block_ids)
    rounded = panel.astype(jnp.bfloat16)
    finished = jnp.dot(rounded, inverse, preferred_element_type=jnp.float32).astype(jnp.bfloat16)
    trailing = rounded[:NT]
    return slab - jnp.dot(finished, trailing.T, preferred_element_type=jnp.float32)
```

```python
import jax
import jax.numpy as jnp
from jax import lax
from jax.experimental import pallas as pl
from jax.experimental.pallas import tpu as pltpu
from jax.sharding import PartitionSpec as P

X, ZL, Y, ZH, CORES = 4, 8, 4, 4, 2
OWN, EXTRA, SURPLUS = 4, 3, 3
BW = 128
W0, W1 = OWN * BW, EXTRA * BW
ROWS, SHARE, PANEL = 256, 32, 1024
SEG = PANEL // ZH
BLK, PIECE = 64, 16
OWNERS, FIRST_OWNER = 4, 2
F32, BF16 = jnp.float32, jnp.bfloat16


def nt_dot(a, b):
    return lax.dot_general(a, b, (((1,), (1,)), ((), ())), preferred_element_type=F32)


def kernel(
    counts, index, table, border, inverse, slab, out,
    kept, parcels, arrived, h0, h1, part, xin, xsum, zin, own, zg, full, trail, inv, acc,
    send_sems, inv_sem, head_sem, body_sem, z_sems, y_sems, c_sems,
    xr_sems, zr_sems, zg_sems, xg_sems, tz_sems, tc_sems,
):
    sc, rw = lax.axis_index("scen"), lax.axis_index("row")
    x, zl = sc % X, sc // X
    y, zh, c = rw // (ZH * CORES), (rw // CORES) % ZH, rw % CORES

    def dev(x_=x, zl_=zl, y_=y, zh_=zh, c_=c):
        return (zl_ * X + x_, (y_ * ZH + zh_) * CORES + c_)

    def xp(d):
        return (x + d) % X

    def yp(d):
        return (y + d) % Y

    def zp(d):
        return (zh + d + ZH) % ZH

    pending = []

    def send(src, dst, sem, target, pred=None):
        copy = pltpu.make_async_remote_copy(
            src_ref=src, dst_ref=dst, send_sem=send_sems.at[len(pending)], recv_sem=sem,
            device_id=target, device_id_type=pl.DeviceIdType.MESH,
        )
        pending.append((pred, copy))
        if pred is None:
            copy.start()
        else:
            pl.when(pred)(copy.start)

    def keep(src, dst, sem, pred):
        copy = pltpu.make_async_copy(src, dst, sem)
        pl.when(pred)(copy.start)

    def arrive(ref, sem):
        pltpu.make_async_copy(ref, ref, sem).wait()

    barrier = pltpu.get_barrier_semaphore()
    peers = [dev(x_=xp(d), c_=cc) for d in range(1, X) for cc in range(CORES)]
    peers += [dev(c_=1 - c)]
    peers += [dev(zl_=(zl + d) % ZL) for d in range(1, ZL)]
    peers += [dev(zh_=zp(1)), dev(zh_=zp(-1))]
    peers += [dev(y_=yp(d)) for d in range(1, Y)]
    for peer in peers:
        pl.semaphore_signal(barrier, inc=1, device_id=peer, device_id_type=pl.DeviceIdType.MESH)

    inv_copies = [
        pltpu.make_async_copy(inverse.at[:, b], inv.at[b], inv_sem.at[b]) for b in range(ZH)
    ]
    for copy in inv_copies:
        copy.start()

    indices = index[...]
    high, low = indices // BW, indices % BW
    weights = jnp.zeros(indices.shape, F32)
    for h in range(table.shape[0]):
        row = jnp.broadcast_to(table[h : h + 1, :], indices.shape)
        picked = jnp.take_along_axis(row, low, axis=1, mode="promise_in_bounds")
        weights = jnp.where(high == h, picked, weights)
    slots = lax.broadcasted_iota(jnp.int32, indices.shape, 0)
    weights = jnp.where(slots < counts[sc], weights, 0.0)

    def scaled(k, first, last):
        rows = border[k, first:last, :].astype(F32)
        return (rows * weights[k : k + 1, :]).astype(BF16)

    def lanes(k):
        return slice(k * BW, (k + 1) * BW)

    for k in range(OWN):
        h0[zh, y, c, :, lanes(k)] = scaled(k, 0, SHARE)
    for o in range(SURPLUS):
        for e in range(EXTRA):
            parcels[o, 0:SHARE, lanes(e)] = scaled(OWN + EXTRA * (o + 1) + e, 0, SHARE)
    pl.semaphore_wait(barrier, len(peers))

    heads = ((h0, 0), (h1, 1))
    halves = ((0, PIECE), (PIECE, SHARE))

    def z_start(h, k):
        for a, step in ((0, 1), (1, -1), (1, 1), (0, -1)):
            lo, hi = halves[a]
            ref = h.at[zh, y, c, lo:hi]
            send(ref, ref, z_sems.at[k, a, 0 if step == 1 else 1], dev(zh_=zp(step)))

    def z_relay(h, k):
        for a, step in ((0, 1), (1, -1)):
            lo, hi = halves[a]
            ref = h.at[zp(-step), y, c, lo:hi]
            arrive(ref, z_sems.at[k, a, 0 if step == 1 else 1])
            send(ref, ref, z_sems.at[k, a, 2], dev(zh_=zp(step)))

    def z_rest(h, k, origin):
        if origin == 2:
            for a in range(2):
                lo, hi = halves[a]
                arrive(h.at[zp(2), y, c, lo:hi], z_sems.at[k, a, 2])
        else:
            a, way = (1, 0) if origin == -1 else (0, 1)
            lo, hi = halves[a]
            arrive(h.at[zp(origin), y, c, lo:hi], z_sems.at[k, a, way])

    origins = (0, -1, 1, 2)

    def y_start(h, k, n):
        ref = h.at[zp(origins[n]), y, c]
        for d in (1, 3, 2):
            send(ref, ref, y_sems.at[k, n], dev(y_=yp(d)))

    def c_start(h, k, n):
        z = zp(origins[n])
        arrive(h.at[z, 0 : Y - 1, 0], y_sems.at[k, n])
        ref = h.at[z, :, c]
        send(ref, ref, c_sems.at[k, n], dev(c_=1 - c))

    z_start(h0, 0)
    for o in range(SURPLUS):
        send(parcels.at[o, 0:SHARE], arrived.at[o, 0:SHARE], head_sem, dev(x_=xp(o + 1)))
    y_start(h0, 0, 0)
    for o in range(SURPLUS):
        for e in range(EXTRA):
            parcels[o, SHARE:ROWS, lanes(e)] = scaled(OWN + EXTRA * (o + 1) + e, SHARE, ROWS)
        send(parcels.at[o, SHARE:ROWS], arrived.at[o, SHARE:ROWS], body_sem, dev(x_=xp(o + 1)))

    def with_parcels(first, last):
        mine = [scaled(OWN + e, first, last) for e in range(EXTRA)]
        total = jnp.concatenate(mine, axis=1)
        for o in range(SURPLUS):
            total = total + arrived[o, first:last, :]
        return total

    arrive(arrived.at[:, 0:SHARE], head_sem)
    extra_heads = with_parcels(0, SHARE)
    h1[zh, y, c] = extra_heads
    kept[0:SHARE, W0 : W0 + W1] = extra_heads
    z_start(h1, 1)
    y_start(h1, 1, 0)
    for k in range(OWN):
        kept[:, lanes(k)] = scaled(k, 0, ROWS)
    arrive(arrived.at[:, SHARE:ROWS], body_sem)
    kept[SHARE:ROWS, W0 : W0 + W1] = with_parcels(SHARE, ROWS)
    c_start(h0, 0, 0)
    c_start(h1, 1, 0)

    left = x // CORES
    upper = x % CORES

    def product(n):
        z = zp(origins[n])
        for h, k in heads:
            arrive(h.at[z, :, 1 - c], c_sems.at[k, n])
        a = h0[z].reshape(SEG, W0)
        b = h1[z].reshape(SEG, W1)
        block = nt_dot(kept[:, 0:W0], a) + nt_dot(kept[:, W0 : W0 + W1], b)
        part[n] = block.astype(BF16).reshape(4, BLK, SEG)
        for b in range(4):
            half, g = b // 2, b % 2
            tx = 2 * c + half
            here = jnp.logical_and(tx == x, g == c)
            dst = xin.at[n, x]
            send(part.at[n, b], dst, xr_sems.at[n], dev(x_=tx, c_=g), jnp.logical_not(here))
            keep(part.at[n, b], dst, xr_sems.at[n], here)

    def x_reduce(n):
        arrive(xin.at[n], xr_sems.at[n])
        total = xin[n, 0].astype(F32)
        for s in range(1, X):
            total = total + xin[n, s].astype(F32)
        xsum[n] = total.astype(BF16).reshape(OWNERS, PIECE, SEG)
        for j in range(OWNERS):
            here = zl == FIRST_OWNER + j
            dst = zin.at[n, zl]
            target = dev(zl_=FIRST_OWNER + j)
            send(xsum.at[n, j], dst, zr_sems.at[n], target, jnp.logical_not(here))
            keep(xsum.at[n, j], dst, zr_sems.at[n], here)

    owner = jnp.logical_and(zl >= FIRST_OWNER, zl < FIRST_OWNER + OWNERS)
    seat = jnp.clip(zl - FIRST_OWNER, 0, OWNERS - 1)

    def z_reduce(n):
        @pl.when(owner)
        def _():
            arrive(zin.at[n], zr_sems.at[n])
            total = zin[n, 0].astype(F32)
            for s in range(1, ZL):
                total = total + zin[n, s].astype(F32)
            own[n] = total.astype(BF16)

        dst = zg.at[n, seat]
        for d in range(1, ZL):
            send(own.at[n], dst, zg_sems.at[n], dev(zl_=(zl + d) % ZL), owner)
        keep(own.at[n], dst, zg_sems.at[n], owner)

    def x_gather(n):
        arrive(zg.at[n], zg_sems.at[n])
        dst = full.at[n, 2 * upper + c]
        for d in range(1, X):
            send(zg.at[n], dst, xg_sems.at[n], dev(x_=xp(d), c_=left))
        send(zg.at[n], dst, xg_sems.at[n], dev(c_=1 - c), left != c)
        keep(zg.at[n], dst, xg_sems.at[n], left == c)

    on_line = y == zl // ZH
    lag = (zh - zl % ZH + ZH) % ZH

    def t_segment(n):
        return (zl % ZH + origins[n] + ZH) % ZH

    def t_source(n):
        source = jnp.logical_and(on_line, lag == 0)
        dst = trail.at[t_segment(n), c]
        send(zg.at[n], dst, tz_sems.at[n], dev(zh_=zp(1)), source)
        send(zg.at[n], dst, tz_sems.at[n], dev(zh_=zp(-1)), source)
        keep(zg.at[n], dst, tz_sems.at[n], source)

    def t_spread(n):
        ref = trail.at[t_segment(n), c]
        arrive(ref, tz_sems.at[n])
        for a, step, at in ((0, 1, 1), (1, -1, 3)):
            cut = trail.at[t_segment(n), c, 2 * a : 2 * a + 2]
            pred = jnp.logical_and(on_line, lag == at)
            send(cut, cut, tz_sems.at[n], dev(zh_=zp(step)), pred)
        for d in (1, 3, 2):
            send(ref, ref, tz_sems.at[n], dev(y_=yp(d)), on_line)
        send(ref, ref, tc_sems.at[n], dev(c_=1 - c))

    def finish_part(n):
        if n == 0:
            for copy in inv_copies:
                copy.wait()
        arrive(full.at[n], xg_sems.at[n])
        step = jnp.dot(
            full[n].reshape(ROWS, SEG), inv[zp(origins[n])].reshape(SEG, PANEL),
            preferred_element_type=F32,
        )
        if n == 0:
            acc[...] = step
        else:
            acc[...] += step

    product(0)
    z_relay(h0, 0)
    z_rest(h0, 0, -1)
    y_start(h0, 0, 1)
    z_rest(h0, 0, 1)
    y_start(h0, 0, 2)
    x_reduce(0)
    z_relay(h1, 1)
    z_rest(h1, 1, -1)
    y_start(h1, 1, 1)
    z_rest(h1, 1, 1)
    y_start(h1, 1, 2)
    c_start(h0, 0, 1)
    c_start(h0, 0, 2)
    c_start(h1, 1, 1)
    c_start(h1, 1, 2)
    product(1)
    product(2)
    z_reduce(0)
    z_rest(h0, 0, 2)
    y_start(h0, 0, 3)
    z_rest(h1, 1, 2)
    y_start(h1, 1, 3)
    x_reduce(1)
    x_reduce(2)
    c_start(h0, 0, 3)
    c_start(h1, 1, 3)
    product(3)
    x_gather(0)
    t_source(0)
    z_reduce(1)
    z_reduce(2)
    x_reduce(3)
    for n in (1, 2):
        x_gather(n)
        t_source(n)
    z_reduce(3)
    for n in range(3):
        finish_part(n)
    x_gather(3)
    t_source(3)
    t_spread(0)
    t_spread(1)
    t_spread(2)
    finish_part(3)
    finished = acc[...].astype(BF16)
    t_spread(3)
    for n in range(4):
        arrive(trail.at[t_segment(n), 1 - c], tc_sems.at[n])
    segments = [trail[b].reshape(2 * BLK, SEG).astype(F32) for b in range(ZH)]
    update = jnp.zeros(out.shape, F32)
    for yy in range(Y):
        for pair in range(ZH // 2):
            cut = slice(yy * BLK, (yy + 1) * BLK)
            columns = jnp.concatenate([segments[2 * pair][:, cut], segments[2 * pair + 1][:, cut]], axis=1)
            at = (yy * (ZH // 2) + pair) * BW
            update = update + nt_dot(finished[:, at : at + BW], columns.astype(BF16))
    out[...] = slab[...] - update

    for pred, copy in pending:
        if pred is None:
            copy.wait_send()
        else:
            pl.when(pred)(copy.wait_send)


def body(border, col_index, barrier, counts, inverse, slab):
    vmem = pl.BlockSpec(memory_space=pltpu.VMEM)
    dma = pltpu.SemaphoreType.DMA
    return pl.pallas_call(
        kernel,
        out_shape=jax.ShapeDtypeStruct(slab.shape, slab.dtype),
        in_specs=[
            pl.BlockSpec(memory_space=pltpu.SMEM), vmem, vmem, vmem,
            pl.BlockSpec(memory_space=pl.ANY), vmem,
        ],
        out_specs=vmem,
        scratch_shapes=[
            pltpu.VMEM((ROWS, W0 + W1), BF16),
            pltpu.VMEM((SURPLUS, ROWS, W1), BF16),
            pltpu.VMEM((SURPLUS, ROWS, W1), BF16),
            pltpu.VMEM((ZH, Y, CORES, SHARE, W0), BF16),
            pltpu.VMEM((ZH, Y, CORES, SHARE, W1), BF16),
            pltpu.VMEM((ZH, 4, BLK, SEG), BF16),
            pltpu.VMEM((ZH, X, BLK, SEG), BF16),
            pltpu.VMEM((ZH, OWNERS, PIECE, SEG), BF16),
            pltpu.VMEM((ZH, ZL, PIECE, SEG), BF16),
            pltpu.VMEM((ZH, PIECE, SEG), BF16),
            pltpu.VMEM((ZH, OWNERS, PIECE, SEG), BF16),
            pltpu.VMEM((ZH, 4, OWNERS, PIECE, SEG), BF16),
            pltpu.VMEM((ZH, CORES, OWNERS, PIECE, SEG), BF16),
            pltpu.VMEM((ZH, Y, BLK, PANEL), BF16),
            pltpu.VMEM((ROWS, PANEL), F32),
            dma((164,)), dma((ZH,)), dma, dma, dma((2, 2, 3)), dma((2, 4)), dma((2, 4)),
            dma((4,)), dma((4,)), dma((4,)), dma((4,)), dma((4,)), dma((4,)),
        ],
        compiler_params=pltpu.CompilerParams(
            collective_id=0, has_side_effects=True, vmem_limit_bytes=48 * 1024 * 1024
        ),
        name="panel_update",
    )(
        counts, col_index, barrier.reshape(-1, BW), border,
        inverse.reshape(Y, ZH, BLK, PANEL), slab,
    )


def solution(mesh):
    return jax.shard_map(
        body,
        mesh=mesh,
        in_specs=(P("scen", "row", None), P("scen", None), P(), P(), P(), P("row", "scen")),
        out_specs=P("row", "scen"),
        check_vma=False,
    )
```

```python
import jax
import jax.numpy as jnp
from jax import lax
from jax.experimental import pallas as pl
from jax.experimental.pallas import tpu as pltpu
from jax.sharding import PartitionSpec as P

X, ZL, Y, ZH, CORES = 4, 8, 4, 4, 2
OWN, EXTRA, SURPLUS = 4, 3, 3
BW = 128
W0, W1 = OWN * BW, EXTRA * BW
ROWS, SHARE, PANEL = 256, 32, 1024
SEG = PANEL // ZH
BLK, PIECE = 64, 16
OWNERS, FIRST_OWNER = 4, 2
F32, BF16 = jnp.float32, jnp.bfloat16


def nt_dot(a, b):
    return lax.dot_general(a, b, (((1,), (1,)), ((), ())), preferred_element_type=F32)


def kernel(
    counts_in, index_in, table_in, border_in, inverse, slab_in, out,
    counts, index, table, border, slab, kept, parcels, arrived, h0, h1, part, xin, xsum, zin, own, zg, full, trail, inv, acc,
    send_sems, in_sems, inv_sem, head_sem, body_sem, z_sems, y_sems, c_sems,
    xr_sems, zr_sems, zg_sems, xg_sems, tz_sems, tc_sems, below_sem, above_sem,
):
    sc, rw = lax.axis_index("scen"), lax.axis_index("row")
    x, zl = sc % X, sc // X
    y, zh, c = rw // (ZH * CORES), (rw // CORES) % ZH, rw % CORES

    def dev(x_=x, zl_=zl, y_=y, zh_=zh, c_=c):
        return (zl_ * X + x_, (y_ * ZH + zh_) * CORES + c_)

    def xp(d):
        return (x + d) % X

    def yp(d):
        return (y + d) % Y

    def zp(d):
        return (zh + d + ZH) % ZH

    pending = []

    def send(src, dst, sem, target, pred=None):
        copy = pltpu.make_async_remote_copy(
            src_ref=src, dst_ref=dst, send_sem=send_sems.at[len(pending)], recv_sem=sem,
            device_id=target, device_id_type=pl.DeviceIdType.MESH,
        )
        pending.append((pred, copy))
        if pred is None:
            copy.start()
        else:
            pl.when(pred)(copy.start)

    def keep(src, dst, sem, pred):
        copy = pltpu.make_async_copy(src, dst, sem)
        pl.when(pred)(copy.start)

    def arrive(ref, sem):
        pltpu.make_async_copy(ref, ref, sem).wait()

    loads = [
        pltpu.make_async_copy(source, target, in_sems.at[n])
        for n, (source, target) in enumerate((
            (index_in, index), (table_in, table), (counts_in, counts),
            (border_in.at[:, 0:SHARE], border.at[:, 0:SHARE]),
            (border_in.at[:, SHARE:ROWS], border.at[:, SHARE:ROWS]),
            (slab_in, slab),
        ))
    ]
    for copy in loads:
        copy.start()

    barrier = pltpu.get_barrier_semaphore()
    peers = [dev(x_=xp(d), c_=cc) for d in range(1, X) for cc in range(CORES)]
    peers += [dev(c_=1 - c)]
    peers += [dev(zh_=zp(1)), dev(zh_=zp(-1))]
    peers += [dev(y_=yp(d)) for d in range(1, Y)]
    mesh_id = pl.DeviceIdType.MESH
    for peer in peers:
        pl.semaphore_signal(barrier, inc=1, device_id=peer, device_id_type=mesh_id)
    up, down = zl < ZL - 1, zl > 0
    for pred, step in ((up, 1), (down, -1)):
        @pl.when(pred)
        def _(step=step):
            target = dev(zl_=zl + step)
            pl.semaphore_signal(barrier, inc=1, device_id=target, device_id_type=mesh_id)

    inv_copies = [
        pltpu.make_async_copy(inverse.at[:, b], inv.at[b], inv_sem.at[b]) for b in range(ZH)
    ]
    for copy in inv_copies:
        copy.start()

    for copy in loads[0:3]:
        copy.wait()
    indices = index[...]
    high, low = indices // BW, indices % BW
    weights = jnp.zeros(indices.shape, F32)
    for h in range(table.shape[0]):
        row = jnp.broadcast_to(table[h : h + 1, :], indices.shape)
        picked = jnp.take_along_axis(row, low, axis=1, mode="promise_in_bounds")
        weights = jnp.where(high == h, picked, weights)
    slots = lax.broadcasted_iota(jnp.int32, indices.shape, 0)
    weights = jnp.where(slots < counts[sc], weights, 0.0)

    def scaled(k, first, last):
        rows = border[k, first:last, :].astype(F32)
        return (rows * weights[k : k + 1, :]).astype(BF16)

    def lanes(k):
        return slice(k * BW, (k + 1) * BW)

    loads[3].wait()
    for k in range(OWN):
        h0[zh, y, c, :, lanes(k)] = scaled(k, 0, SHARE)
    for o in range(SURPLUS):
        for e in range(EXTRA):
            parcels[o, 0:SHARE, lanes(e)] = scaled(OWN + EXTRA * (o + 1) + e, 0, SHARE)
    near = up.astype(jnp.int32) + down.astype(jnp.int32)
    pl.semaphore_wait(barrier, len(peers) + near)

    heads = ((h0, 0), (h1, 1))
    halves = ((0, PIECE), (PIECE, SHARE))

    def z_start(h, k):
        for a, step in ((0, 1), (1, -1), (1, 1), (0, -1)):
            lo, hi = halves[a]
            ref = h.at[zh, y, c, lo:hi]
            send(ref, ref, z_sems.at[k, a, 0 if step == 1 else 1], dev(zh_=zp(step)))

    def z_relay(h, k):
        for a, step in ((0, 1), (1, -1)):
            lo, hi = halves[a]
            ref = h.at[zp(-step), y, c, lo:hi]
            arrive(ref, z_sems.at[k, a, 0 if step == 1 else 1])
            send(ref, ref, z_sems.at[k, a, 2], dev(zh_=zp(step)))

    def z_rest(h, k, origin):
        if origin == 2:
            for a in range(2):
                lo, hi = halves[a]
                arrive(h.at[zp(2), y, c, lo:hi], z_sems.at[k, a, 2])
        else:
            a, way = (1, 0) if origin == -1 else (0, 1)
            lo, hi = halves[a]
            arrive(h.at[zp(origin), y, c, lo:hi], z_sems.at[k, a, way])

    origins = (0, -1, 1, 2)

    def y_start(h, k, n):
        ref = h.at[zp(origins[n]), y, c]
        for d in (1, 3, 2):
            send(ref, ref, y_sems.at[k, n], dev(y_=yp(d)))

    def c_start(h, k, n):
        z = zp(origins[n])
        arrive(h.at[z, 0 : Y - 1, 0], y_sems.at[k, n])
        ref = h.at[z, :, c]
        send(ref, ref, c_sems.at[k, n], dev(c_=1 - c))

    z_start(h0, 0)
    for o in range(SURPLUS):
        send(parcels.at[o, 0:SHARE], arrived.at[o, 0:SHARE], head_sem, dev(x_=xp(o + 1)))
    y_start(h0, 0, 0)
    loads[4].wait()
    for o in range(SURPLUS):
        for e in range(EXTRA):
            parcels[o, SHARE:ROWS, lanes(e)] = scaled(OWN + EXTRA * (o + 1) + e, SHARE, ROWS)
        send(parcels.at[o, SHARE:ROWS], arrived.at[o, SHARE:ROWS], body_sem, dev(x_=xp(o + 1)))

    def with_parcels(first, last):
        mine = [scaled(OWN + e, first, last) for e in range(EXTRA)]
        total = jnp.concatenate(mine, axis=1)
        for o in range(SURPLUS):
            total = total + arrived[o, first:last, :]
        return total

    arrive(arrived.at[:, 0:SHARE], head_sem)
    extra_heads = with_parcels(0, SHARE)
    h1[zh, y, c] = extra_heads
    kept[0:SHARE, W0 : W0 + W1] = extra_heads
    z_start(h1, 1)
    y_start(h1, 1, 0)

    for wait_if, send_if, step, sem in ((down, up, 1, below_sem), (up, down, -1, above_sem)):
        @pl.when(wait_if)
        def _(sem=sem):
            pl.semaphore_wait(sem, 1)

        @pl.when(send_if)
        def _(step=step, sem=sem):
            target = dev(zl_=zl + step)
            pl.semaphore_signal(sem, inc=1, device_id=target, device_id_type=mesh_id)

    for k in range(OWN):
        kept[:, lanes(k)] = scaled(k, 0, ROWS)

    left = x // CORES
    upper = x % CORES

    def product(n):
        z = zp(origins[n])
        for h, k in heads:
            arrive(h.at[z, :, 1 - c], c_sems.at[k, n])
        a = h0[z].reshape(SEG, W0)
        b = h1[z].reshape(SEG, W1)
        block = nt_dot(kept[:, 0:W0], a) + nt_dot(kept[:, W0 : W0 + W1], b)
        part[n] = block.astype(BF16).reshape(4, BLK, SEG)
        for b in range(4):
            half, g = b // 2, b % 2
            tx = 2 * c + half
            here = jnp.logical_and(tx == x, g == c)
            dst = xin.at[n, x]
            send(part.at[n, b], dst, xr_sems.at[n], dev(x_=tx, c_=g), jnp.logical_not(here))
            keep(part.at[n, b], dst, xr_sems.at[n], here)

    def x_reduce(n):
        arrive(xin.at[n], xr_sems.at[n])
        total = xin[n, 0].astype(F32)
        for s in range(1, X):
            total = total + xin[n, s].astype(F32)
        xsum[n] = total.astype(BF16).reshape(OWNERS, PIECE, SEG)
        for j in range(OWNERS):
            here = zl == FIRST_OWNER + j
            dst = zin.at[n, zl]
            target = dev(zl_=FIRST_OWNER + j)
            send(xsum.at[n, j], dst, zr_sems.at[n], target, jnp.logical_not(here))
            keep(xsum.at[n, j], dst, zr_sems.at[n], here)

    owner = jnp.logical_and(zl >= FIRST_OWNER, zl < FIRST_OWNER + OWNERS)
    seat = jnp.clip(zl - FIRST_OWNER, 0, OWNERS - 1)

    def z_reduce(n):
        @pl.when(owner)
        def _():
            arrive(zin.at[n], zr_sems.at[n])
            total = zin[n, 0].astype(F32)
            for s in range(1, ZL):
                total = total + zin[n, s].astype(F32)
            own[n] = total.astype(BF16)

        dst = zg.at[n, seat]
        for d in range(1, ZL):
            send(own.at[n], dst, zg_sems.at[n], dev(zl_=(zl + d) % ZL), owner)
        keep(own.at[n], dst, zg_sems.at[n], owner)

    def x_gather(n):
        arrive(zg.at[n], zg_sems.at[n])
        dst = full.at[n, 2 * upper + c]
        for d in range(1, X):
            send(zg.at[n], dst, xg_sems.at[n], dev(x_=xp(d), c_=left))
        send(zg.at[n], dst, xg_sems.at[n], dev(c_=1 - c), left != c)
        keep(zg.at[n], dst, xg_sems.at[n], left == c)

    on_line = y == zl // ZH
    source = jnp.logical_and(on_line, zh == zl % ZH)

    def t_segment(n, origin):
        return (origin + origins[n] + ZH) % ZH

    def t_send(n):
        pred = jnp.logical_and(owner, y < ZL // ZH)
        dst = trail.at[t_segment(n, zh), c, seat]
        for d in (2, 1, 3):
            send(own.at[n], dst, tz_sems.at[n], dev(zl_=(y * ZH + zh) % ZL, zh_=zp(d)), pred)

    def t_keep(n):
        keep(zg.at[n], trail.at[t_segment(n, zh), c], tz_sems.at[n], source)

    def t_spread(n):
        ref = trail.at[t_segment(n, zl % ZH), c]
        arrive(ref, tz_sems.at[n])
        for d in (1, 3, 2):
            send(ref, ref, tz_sems.at[n], dev(y_=yp(d)), on_line)
        send(ref, ref, tc_sems.at[n], dev(c_=1 - c))

    def finish_part(n):
        if n == 0:
            for copy in inv_copies:
                copy.wait()
        arrive(full.at[n], xg_sems.at[n])
        step = jnp.dot(
            full[n].reshape(ROWS, SEG), inv[zp(origins[n])].reshape(SEG, PANEL),
            preferred_element_type=F32,
        )
        if n == 0:
            acc[...] = step
        else:
            acc[...] += step

    def relay(h, k):
        z_relay(h, k)
        z_rest(h, k, -1)
        y_start(h, k, 1)
        z_rest(h, k, 1)
        y_start(h, k, 2)

    c_start(h0, 0, 0)
    c_start(h1, 1, 0)
    relay(h0, 0)
    arrive(arrived.at[:, SHARE:ROWS], body_sem)
    kept[SHARE:ROWS, W0 : W0 + W1] = with_parcels(SHARE, ROWS)
    product(0)
    relay(h1, 1)
    x_reduce(0)
    for n in (1, 2):
        c_start(h0, 0, n)
        c_start(h1, 1, n)
    product(1)
    product(2)
    for h, k in heads:
        z_rest(h, k, 2)
        y_start(h, k, 3)
    z_reduce(0)
    t_send(0)
    x_reduce(1)
    x_reduce(2)
    c_start(h0, 0, 3)
    c_start(h1, 1, 3)
    product(3)
    for n in (1, 2):
        z_reduce(n)
        t_send(n)
    x_reduce(3)
    for n in range(3):
        x_gather(n)
        t_keep(n)
    z_reduce(3)
    t_send(3)
    for n in range(3):
        finish_part(n)
    x_gather(3)
    t_keep(3)
    for n in range(4):
        t_spread(n)
    finish_part(3)
    finished = acc[...].astype(BF16)
    for n in range(4):
        arrive(trail.at[t_segment(n, zl % ZH), 1 - c], tc_sems.at[n])
    segments = [trail[b].reshape(2 * BLK, SEG).astype(F32) for b in range(ZH)]
    update = jnp.zeros(out.shape, F32)
    for yy in range(Y):
        for pair in range(ZH // 2):
            cut = slice(yy * BLK, (yy + 1) * BLK)
            columns = jnp.concatenate([segments[2 * pair][:, cut], segments[2 * pair + 1][:, cut]], axis=1)
            at = (yy * (ZH // 2) + pair) * BW
            update = update + nt_dot(finished[:, at : at + BW], columns.astype(BF16))
    loads[5].wait()
    out[...] = slab[...] - update

    for pred, copy in pending:
        if pred is None:
            copy.wait_send()
        else:
            pl.when(pred)(copy.wait_send)


def body(border, col_index, barrier, counts, inverse, slab):
    vmem = pl.BlockSpec(memory_space=pltpu.VMEM)
    dma = pltpu.SemaphoreType.DMA
    return pl.pallas_call(
        kernel,
        out_shape=jax.ShapeDtypeStruct(slab.shape, slab.dtype),
        in_specs=[pl.BlockSpec(memory_space=pl.ANY)] * 6,
        out_specs=vmem,
        scratch_shapes=[
            pltpu.SMEM(counts.shape, counts.dtype),
            pltpu.VMEM(col_index.shape, col_index.dtype),
            pltpu.VMEM((barrier.shape[0] // BW, BW), barrier.dtype),
            pltpu.VMEM(border.shape, border.dtype),
            pltpu.VMEM(slab.shape, slab.dtype),
            pltpu.VMEM((ROWS, W0 + W1), BF16),
            pltpu.VMEM((SURPLUS, ROWS, W1), BF16),
            pltpu.VMEM((SURPLUS, ROWS, W1), BF16),
            pltpu.VMEM((ZH, Y, CORES, SHARE, W0), BF16),
            pltpu.VMEM((ZH, Y, CORES, SHARE, W1), BF16),
            pltpu.VMEM((ZH, 4, BLK, SEG), BF16),
            pltpu.VMEM((ZH, X, BLK, SEG), BF16),
            pltpu.VMEM((ZH, OWNERS, PIECE, SEG), BF16),
            pltpu.VMEM((ZH, ZL, PIECE, SEG), BF16),
            pltpu.VMEM((ZH, PIECE, SEG), BF16),
            pltpu.VMEM((ZH, OWNERS, PIECE, SEG), BF16),
            pltpu.VMEM((ZH, 4, OWNERS, PIECE, SEG), BF16),
            pltpu.VMEM((ZH, CORES, OWNERS, PIECE, SEG), BF16),
            pltpu.VMEM((ZH, Y, BLK, PANEL), BF16),
            pltpu.VMEM((ROWS, PANEL), F32),
            dma((164,)), dma((6,)), dma((ZH,)), dma, dma, dma((2, 2, 3)), dma((2, 4)), dma((2, 4)),
            dma((4,)), dma((4,)), dma((4,)), dma((4,)), dma((4,)), dma((4,)),
            pltpu.SemaphoreType.REGULAR, pltpu.SemaphoreType.REGULAR,
        ],
        compiler_params=pltpu.CompilerParams(
            collective_id=0, has_side_effects=True, vmem_limit_bytes=67043328
        ),
        name="panel_update",
    )(
        counts, col_index, barrier.reshape(-1, BW), border,
        inverse.reshape(Y, ZH, BLK, PANEL), slab,
    )


def solution(mesh):
    return jax.shard_map(
        body,
        mesh=mesh,
        in_specs=(P("scen", "row", None), P("scen", None), P(), P(), P(), P("row", "scen")),
        out_specs=P("row", "scen"),
        check_vma=False,
    )
```

```python
import jax
import jax.numpy as jnp
from jax import lax
from jax.experimental import pallas as pl
from jax.experimental.pallas import tpu as pltpu
from jax.sharding import PartitionSpec as P

X, ZL, Y, ZH, CORES = 4, 8, 4, 4, 2
OWN, EXTRA, SURPLUS = 4, 3, 3
BW = 128
W0, W1 = OWN * BW, EXTRA * BW
ROWS, SHARE, PANEL = 256, 32, 1024
SEG = PANEL // ZH
BLK, PIECE = 64, 16
OWNERS, FIRST_OWNER = 4, 2
F32, BF16 = jnp.float32, jnp.bfloat16


def nt_dot(a, b):
    return lax.dot_general(a, b, (((1,), (1,)), ((), ())), preferred_element_type=F32)


def kernel(
    counts_in, index_in, table_in, border_in, inverse, slab_in, out,
    counts, index, table, border, slab, kept, parcels, arrived, h0, h1, part, xin, xsum, zin, own, zg, full, trail, inv, acc,
    send_sems, in_sems, inv_sem, head_sem, body_sem, z_sems, y_sems, c_sems,
    xr_sems, zr_sems, zg_sems, xg_sems, tz_sems, tc_sems, below_sem, above_sem,
):
    sc, rw = lax.axis_index("scen"), lax.axis_index("row")
    x, zl = sc % X, sc // X
    y, zh, c = rw // (ZH * CORES), (rw // CORES) % ZH, rw % CORES

    def dev(x_=x, zl_=zl, y_=y, zh_=zh, c_=c):
        return (zl_ * X + x_, (y_ * ZH + zh_) * CORES + c_)

    def xp(d):
        return (x + d) % X

    def yp(d):
        return (y + d) % Y

    def zp(d):
        return (zh + d + ZH) % ZH

    pending = []

    def send(src, dst, sem, target, pred=None):
        copy = pltpu.make_async_remote_copy(
            src_ref=src, dst_ref=dst, send_sem=send_sems.at[len(pending)], recv_sem=sem,
            device_id=target, device_id_type=pl.DeviceIdType.MESH,
        )
        pending.append((pred, copy))
        if pred is None:
            copy.start()
        else:
            pl.when(pred)(copy.start)

    def keep(src, dst, sem, pred):
        copy = pltpu.make_async_copy(src, dst, sem)
        pl.when(pred)(copy.start)

    def arrive(ref, sem):
        pltpu.make_async_copy(ref, ref, sem).wait()

    loads = [
        pltpu.make_async_copy(source, target, in_sems.at[n])
        for n, (source, target) in enumerate((
            (index_in, index), (table_in, table), (counts_in, counts),
            (border_in.at[:, 0:SHARE], border.at[:, 0:SHARE]),
            (border_in.at[:, SHARE:ROWS], border.at[:, SHARE:ROWS]),
            (slab_in, slab),
        ))
    ]
    for copy in loads:
        copy.start()

    barrier = pltpu.get_barrier_semaphore()
    peers = [dev(x_=xp(d), c_=cc) for d in range(1, X) for cc in range(CORES)]
    peers += [dev(c_=1 - c)]
    peers += [dev(zh_=zp(1)), dev(zh_=zp(-1))]
    peers += [dev(y_=yp(d)) for d in range(1, Y)]
    mesh_id = pl.DeviceIdType.MESH
    for peer in peers:
        pl.semaphore_signal(barrier, inc=1, device_id=peer, device_id_type=mesh_id)
    up, down = zl < ZL - 1, zl > 0
    for pred, step in ((up, 1), (down, -1)):
        @pl.when(pred)
        def _(step=step):
            target = dev(zl_=zl + step)
            pl.semaphore_signal(barrier, inc=1, device_id=target, device_id_type=mesh_id)

    inv_copies = [
        pltpu.make_async_copy(inverse.at[:, b], inv.at[b], inv_sem.at[b]) for b in range(ZH)
    ]
    for copy in inv_copies:
        copy.start()

    for copy in loads[0:3]:
        copy.wait()
    indices = index[...]
    high, low = indices // BW, indices % BW
    weights = jnp.zeros(indices.shape, F32)
    for h in range(table.shape[0]):
        row = jnp.broadcast_to(table[h : h + 1, :], indices.shape)
        picked = jnp.take_along_axis(row, low, axis=1, mode="promise_in_bounds")
        weights = jnp.where(high == h, picked, weights)
    slots = lax.broadcasted_iota(jnp.int32, indices.shape, 0)
    weights = jnp.where(slots < counts[sc], weights, 0.0)

    def scaled(k, first, last):
        rows = border[k, first:last, :].astype(F32)
        return (rows * weights[k : k + 1, :]).astype(BF16)

    def lanes(k):
        return slice(k * BW, (k + 1) * BW)

    loads[3].wait()
    for k in range(OWN):
        h0[zh, y, c, :, lanes(k)] = scaled(k, 0, SHARE)
    for o in range(SURPLUS):
        for e in range(EXTRA):
            parcels[o, 0:SHARE, lanes(e)] = scaled(OWN + EXTRA * (o + 1) + e, 0, SHARE)
    near = up.astype(jnp.int32) + down.astype(jnp.int32)
    pl.semaphore_wait(barrier, len(peers) + near)

    heads = ((h0, 0), (h1, 1))
    halves = ((0, PIECE), (PIECE, SHARE))

    def z_start(h, k):
        for a, step in ((0, 1), (1, -1), (1, 1), (0, -1)):
            lo, hi = halves[a]
            ref = h.at[zh, y, c, lo:hi]
            send(ref, ref, z_sems.at[k, a, 0 if step == 1 else 1], dev(zh_=zp(step)))

    def z_relay(h, k):
        for a, step in ((0, 1), (1, -1)):
            lo, hi = halves[a]
            ref = h.at[zp(-step), y, c, lo:hi]
            arrive(ref, z_sems.at[k, a, 0 if step == 1 else 1])
            send(ref, ref, z_sems.at[k, a, 2], dev(zh_=zp(step)))

    def z_rest(h, k, origin):
        if origin == 2:
            for a in range(2):
                lo, hi = halves[a]
                arrive(h.at[zp(2), y, c, lo:hi], z_sems.at[k, a, 2])
        else:
            a, way = (1, 0) if origin == -1 else (0, 1)
            lo, hi = halves[a]
            arrive(h.at[zp(origin), y, c, lo:hi], z_sems.at[k, a, way])

    origins = (0, -1, 1, 2)

    def y_start(h, k, n):
        ref = h.at[zp(origins[n]), y, c]
        for d in (1, 3, 2):
            send(ref, ref, y_sems.at[k, n], dev(y_=yp(d)))

    def c_start(h, k, n):
        z = zp(origins[n])
        arrive(h.at[z, 0 : Y - 1, 0], y_sems.at[k, n])
        ref = h.at[z, :, c]
        send(ref, ref, c_sems.at[k, n], dev(c_=1 - c))

    z_start(h0, 0)
    for o in range(SURPLUS):
        send(parcels.at[o, 0:SHARE], arrived.at[o, 0:SHARE], head_sem, dev(x_=xp(o + 1)))
    y_start(h0, 0, 0)
    loads[4].wait()
    for o in range(SURPLUS):
        for e in range(EXTRA):
            parcels[o, SHARE:ROWS, lanes(e)] = scaled(OWN + EXTRA * (o + 1) + e, SHARE, ROWS)
        send(parcels.at[o, SHARE:ROWS], arrived.at[o, SHARE:ROWS], body_sem, dev(x_=xp(o + 1)))

    def with_parcels(first, last):
        mine = [scaled(OWN + e, first, last) for e in range(EXTRA)]
        total = jnp.concatenate(mine, axis=1)
        for o in range(SURPLUS):
            total = total + arrived[o, first:last, :]
        return total

    arrive(arrived.at[:, 0:SHARE], head_sem)
    extra_heads = with_parcels(0, SHARE)
    h1[zh, y, c] = extra_heads
    kept[0:SHARE, W0 : W0 + W1] = extra_heads
    z_start(h1, 1)
    y_start(h1, 1, 0)

    def token(step, sem):
        first, last = (0, ZL - 1) if step == 1 else (ZL - 1, 0)

        @pl.when(zl != first)
        def _():
            pl.semaphore_wait(sem, 1)

        @pl.when(zl != last)
        def _():
            target = dev(zl_=zl + step)
            pl.semaphore_signal(sem, inc=1, device_id=target, device_id_type=mesh_id)

    @pl.when(zl < ZL // 2)
    def _():
        token(1, below_sem)
        token(-1, above_sem)

    @pl.when(zl >= ZL // 2)
    def _():
        token(-1, above_sem)
        token(1, below_sem)

    for k in range(OWN):
        kept[:, lanes(k)] = scaled(k, 0, ROWS)

    left = x // CORES
    upper = x % CORES

    def product(n):
        z = zp(origins[n])
        for h, k in heads:
            arrive(h.at[z, :, 1 - c], c_sems.at[k, n])
        a = h0[z].reshape(SEG, W0)
        b = h1[z].reshape(SEG, W1)
        block = nt_dot(kept[:, 0:W0], a) + nt_dot(kept[:, W0 : W0 + W1], b)
        part[n] = block.astype(BF16).reshape(4, BLK, SEG)
        for b in range(4):
            half, g = b // 2, b % 2
            tx = 2 * c + half
            here = jnp.logical_and(tx == x, g == c)
            dst = xin.at[n, x]
            send(part.at[n, b], dst, xr_sems.at[n], dev(x_=tx, c_=g), jnp.logical_not(here))
            keep(part.at[n, b], dst, xr_sems.at[n], here)

    def x_reduce(n):
        arrive(xin.at[n], xr_sems.at[n])
        total = xin[n, 0].astype(F32)
        for s in range(1, X):
            total = total + xin[n, s].astype(F32)
        xsum[n] = total.astype(BF16).reshape(OWNERS, PIECE, SEG)
        for j in range(OWNERS):
            here = zl == FIRST_OWNER + j
            dst = zin.at[n, zl]
            target = dev(zl_=FIRST_OWNER + j)
            send(xsum.at[n, j], dst, zr_sems.at[n], target, jnp.logical_not(here))
            keep(xsum.at[n, j], dst, zr_sems.at[n], here)

    owner = jnp.logical_and(zl >= FIRST_OWNER, zl < FIRST_OWNER + OWNERS)
    seat = jnp.clip(zl - FIRST_OWNER, 0, OWNERS - 1)

    def z_reduce(n):
        @pl.when(owner)
        def _():
            arrive(zin.at[n], zr_sems.at[n])
            total = zin[n, 0].astype(F32)
            for s in range(1, ZL):
                total = total + zin[n, s].astype(F32)
            own[n] = total.astype(BF16)

        dst = zg.at[n, seat]
        for d in range(1, ZL):
            send(own.at[n], dst, zg_sems.at[n], dev(zl_=(zl + d) % ZL), owner)
        keep(own.at[n], dst, zg_sems.at[n], owner)

    def x_gather(n):
        arrive(zg.at[n], zg_sems.at[n])
        dst = full.at[n, 2 * upper + c]
        for d in range(1, X):
            send(zg.at[n], dst, xg_sems.at[n], dev(x_=xp(d), c_=left))
        send(zg.at[n], dst, xg_sems.at[n], dev(c_=1 - c), left != c)
        keep(zg.at[n], dst, xg_sems.at[n], left == c)

    on_line = y == zl // ZH
    source = jnp.logical_and(on_line, zh == zl % ZH)

    def t_segment(n, origin):
        return (origin + origins[n] + ZH) % ZH

    def t_send(n):
        pred = jnp.logical_and(owner, y < ZL // ZH)
        dst = trail.at[t_segment(n, zh), c, seat]
        for d in (2, 1, 3):
            send(own.at[n], dst, tz_sems.at[n], dev(zl_=(y * ZH + zh) % ZL, zh_=zp(d)), pred)

    def t_keep(n):
        keep(zg.at[n], trail.at[t_segment(n, zh), c], tz_sems.at[n], source)

    def t_spread(n):
        ref = trail.at[t_segment(n, zl % ZH), c]
        arrive(ref, tz_sems.at[n])
        for d in (1, 3, 2):
            send(ref, ref, tz_sems.at[n], dev(y_=yp(d)), on_line)
        send(ref, ref, tc_sems.at[n], dev(c_=1 - c))

    def finish_part(n):
        if n == 0:
            for copy in inv_copies:
                copy.wait()
        arrive(full.at[n], xg_sems.at[n])
        step = jnp.dot(
            full[n].reshape(ROWS, SEG), inv[zp(origins[n])].reshape(SEG, PANEL),
            preferred_element_type=F32,
        )
        if n == 0:
            acc[...] = step
        else:
            acc[...] += step

    def relay(h, k):
        z_relay(h, k)
        z_rest(h, k, -1)
        y_start(h, k, 1)
        z_rest(h, k, 1)
        y_start(h, k, 2)

    c_start(h0, 0, 0)
    c_start(h1, 1, 0)
    relay(h0, 0)
    relay(h1, 1)
    arrive(arrived.at[:, SHARE:ROWS], body_sem)
    kept[SHARE:ROWS, W0 : W0 + W1] = with_parcels(SHARE, ROWS)
    product(0)
    for n in (1, 2):
        c_start(h0, 0, n)
        c_start(h1, 1, n)
    product(1)
    product(2)
    x_reduce(0)
    for h, k in heads:
        z_rest(h, k, 2)
        y_start(h, k, 3)
    x_reduce(1)
    x_reduce(2)
    c_start(h0, 0, 3)
    c_start(h1, 1, 3)
    z_reduce(0)
    t_send(0)
    product(3)
    for n in (1, 2):
        z_reduce(n)
        t_send(n)
    x_reduce(3)
    for n in range(3):
        x_gather(n)
        t_keep(n)
    z_reduce(3)
    t_send(3)
    for n in range(3):
        finish_part(n)
    x_gather(3)
    t_keep(3)
    for n in range(3):
        t_spread(n)
    finish_part(3)
    t_spread(3)
    finished = acc[...].astype(BF16)
    for n in range(4):
        arrive(trail.at[t_segment(n, zl % ZH), 1 - c], tc_sems.at[n])
    segments = [trail[b].reshape(2 * BLK, SEG).astype(F32) for b in range(ZH)]
    update = jnp.zeros(out.shape, F32)
    for yy in range(Y):
        for pair in range(ZH // 2):
            cut = slice(yy * BLK, (yy + 1) * BLK)
            columns = jnp.concatenate([segments[2 * pair][:, cut], segments[2 * pair + 1][:, cut]], axis=1)
            at = (yy * (ZH // 2) + pair) * BW
            update = update + nt_dot(finished[:, at : at + BW], columns.astype(BF16))
    loads[5].wait()
    out[...] = slab[...] - update

    for pred, copy in pending:
        if pred is None:
            copy.wait_send()
        else:
            pl.when(pred)(copy.wait_send)


def body(border, col_index, barrier, counts, inverse, slab):
    vmem = pl.BlockSpec(memory_space=pltpu.VMEM)
    dma = pltpu.SemaphoreType.DMA
    return pl.pallas_call(
        kernel,
        out_shape=jax.ShapeDtypeStruct(slab.shape, slab.dtype),
        in_specs=[pl.BlockSpec(memory_space=pl.ANY)] * 6,
        out_specs=vmem,
        scratch_shapes=[
            pltpu.SMEM(counts.shape, counts.dtype),
            pltpu.VMEM(col_index.shape, col_index.dtype),
            pltpu.VMEM((barrier.shape[0] // BW, BW), barrier.dtype),
            pltpu.VMEM(border.shape, border.dtype),
            pltpu.VMEM(slab.shape, slab.dtype),
            pltpu.VMEM((ROWS, W0 + W1), BF16),
            pltpu.VMEM((SURPLUS, ROWS, W1), BF16),
            pltpu.VMEM((SURPLUS, ROWS, W1), BF16),
            pltpu.VMEM((ZH, Y, CORES, SHARE, W0), BF16),
            pltpu.VMEM((ZH, Y, CORES, SHARE, W1), BF16),
            pltpu.VMEM((ZH, 4, BLK, SEG), BF16),
            pltpu.VMEM((ZH, X, BLK, SEG), BF16),
            pltpu.VMEM((ZH, OWNERS, PIECE, SEG), BF16),
            pltpu.VMEM((ZH, ZL, PIECE, SEG), BF16),
            pltpu.VMEM((ZH, PIECE, SEG), BF16),
            pltpu.VMEM((ZH, OWNERS, PIECE, SEG), BF16),
            pltpu.VMEM((ZH, 4, OWNERS, PIECE, SEG), BF16),
            pltpu.VMEM((ZH, CORES, OWNERS, PIECE, SEG), BF16),
            pltpu.VMEM((ZH, Y, BLK, PANEL), BF16),
            pltpu.VMEM((ROWS, PANEL), F32),
            dma((164,)), dma((6,)), dma((ZH,)), dma, dma, dma((2, 2, 3)), dma((2, 4)), dma((2, 4)),
            dma((4,)), dma((4,)), dma((4,)), dma((4,)), dma((4,)), dma((4,)),
            pltpu.SemaphoreType.REGULAR, pltpu.SemaphoreType.REGULAR,
        ],
        compiler_params=pltpu.CompilerParams(
            collective_id=0, has_side_effects=True, vmem_limit_bytes=67043328
        ),
        name="panel_update",
    )(
        counts, col_index, barrier.reshape(-1, BW), border,
        inverse.reshape(Y, ZH, BLK, PANEL), slab,
    )


def solution(mesh):
    return jax.shard_map(
        body,
        mesh=mesh,
        in_specs=(P("scen", "row", None), P("scen", None), P(), P(), P(), P("row", "scen")),
        out_specs=P("row", "scen"),
        check_vma=False,
    )
```

```python
import jax
import jax.numpy as jnp
from jax import lax
from jax.experimental import pallas as pl
from jax.experimental.pallas import tpu as pltpu
from jax.sharding import PartitionSpec as P

X, ZL, Y, ZH, CORES = 4, 8, 4, 4, 2
OWN, EXTRA, SURPLUS = 4, 3, 3
BW = 128
W0, W1 = OWN * BW, EXTRA * BW
ROWS, SHARE, PANEL, HALF = 256, 32, 1024, 128
SEG = PANEL // ZH
HELD = Y * CORES * ROWS
OWNER_OF = (3, 4, 2, 5)
GROUPS = ((0, 3), (3, 4))
F32, BF16 = jnp.float32, jnp.bfloat16


def nt_dot(a, b):
    return lax.dot_general(a, b, (((1,), (1,)), ((), ())), preferred_element_type=F32)


def tn_dot(a, b):
    return lax.dot_general(a, b, (((0,), (0,)), ((), ())), preferred_element_type=F32)


def kernel(
    counts_in, index_in, table_in, border_in, inverse, slab_in, out,
    counts, index, table, border, slab, parcels, arrived, s0, s1, h0, h1,
    part, xin, xsum, zin, own, zg, full, trail, natural, inv, acc,
    send_sems, in_sems, inv_sem, head_sem, body_sem, s_sems, sc_sems, z_sems,
    xr_sems, zr_sems, zg_sems, xg_sems, tz_sems, ty_sems, tc_sems, below_sem, above_sem,
):
    sc, rw = lax.axis_index("scen"), lax.axis_index("row")
    x, zl = sc % X, sc // X
    y, zh, c = rw // (ZH * CORES), (rw // CORES) % ZH, rw % CORES
    mesh_id = pl.DeviceIdType.MESH

    def dev(x_=x, zl_=zl, y_=y, zh_=zh, c_=c):
        return (zl_ * X + x_, (y_ * ZH + zh_) * CORES + c_)

    def xp(d):
        return (x + d) % X

    def yp(d):
        return (y + d) % Y

    def zp(d):
        return (zh + d + ZH) % ZH

    pending = []

    def send(src, dst, sem, target, pred=None):
        copy = pltpu.make_async_remote_copy(
            src_ref=src, dst_ref=dst, send_sem=send_sems.at[len(pending)], recv_sem=sem,
            device_id=target, device_id_type=mesh_id,
        )
        pending.append((pred, copy))
        if pred is None:
            copy.start()
        else:
            pl.when(pred)(copy.start)

    def keep(src, dst, sem, pred):
        copy = pltpu.make_async_copy(src, dst, sem)
        pl.when(pred)(copy.start)

    def arrive(ref, sem):
        pltpu.make_async_copy(ref, ref, sem).wait()

    loads = [
        pltpu.make_async_copy(source, target, in_sems.at[n])
        for n, (source, target) in enumerate((
            (index_in, index), (table_in, table), (counts_in, counts),
            (border_in.at[:, 0:SHARE], border.at[:, 0:SHARE]),
            (border_in.at[:, SHARE:ROWS], border.at[:, SHARE:ROWS]),
            (slab_in, slab),
        ))
    ]
    for copy in loads:
        copy.start()

    barrier = pltpu.get_barrier_semaphore()
    peers = [dev(x_=xp(d)) for d in range(1, X)] + [dev(y_=yp(d)) for d in range(1, Y)]
    peers += [dev(c_=1 - c), dev(zh_=zp(1)), dev(zh_=zp(-1))]
    for peer in peers:
        pl.semaphore_signal(barrier, inc=1, device_id=peer, device_id_type=mesh_id)
    up, down = zl < ZL - 1, zl > 0
    for pred, step in ((up, 1), (down, -1)):
        @pl.when(pred)
        def _(step=step):
            target = dev(zl_=zl + step)
            pl.semaphore_signal(barrier, inc=1, device_id=target, device_id_type=mesh_id)

    inv_copies = [
        pltpu.make_async_copy(inverse.at[:, b], inv.at[b], inv_sem.at[b]) for b in range(ZH)
    ]
    for copy in inv_copies:
        copy.start()

    for copy in loads[0:3]:
        copy.wait()
    indices = index[...]
    high, low = indices // BW, indices % BW
    weights = jnp.zeros(indices.shape, F32)
    for h in range(table.shape[0]):
        row = jnp.broadcast_to(table[h : h + 1, :], indices.shape)
        picked = jnp.take_along_axis(row, low, axis=1, mode="promise_in_bounds")
        weights = jnp.where(high == h, picked, weights)
    slots = lax.broadcasted_iota(jnp.int32, indices.shape, 0)
    weights = jnp.where(slots < counts[sc], weights, 0.0)

    def scaled(k, first, last):
        rows = border[k, first:last, :].astype(F32)
        return (rows * weights[k : k + 1, :]).astype(BF16)

    def lanes(k):
        return slice(k * BW, (k + 1) * BW)

    loads[3].wait()
    for k in range(OWN):
        h0[zh, :, lanes(k)] = scaled(k, 0, SHARE)
    for o in range(SURPLUS):
        for e in range(EXTRA):
            parcels[o, 0:SHARE, lanes(e)] = scaled(OWN + EXTRA * (o + 1) + e, 0, SHARE)
    near = up.astype(jnp.int32) + down.astype(jnp.int32)
    pl.semaphore_wait(barrier, len(peers) + near)

    heads = ((h0, 0), (h1, 1))
    cuts = ((0, SHARE // 2), (SHARE // 2, SHARE))

    def z_start(h, k):
        for a, step in ((0, 1), (1, -1), (1, 1), (0, -1)):
            lo, hi = cuts[a]
            ref = h.at[zh, lo:hi]
            send(ref, ref, z_sems.at[k, a, 0 if step == 1 else 1], dev(zh_=zp(step)))

    def z_relay(h, k):
        for a, step in ((0, 1), (1, -1)):
            lo, hi = cuts[a]
            ref = h.at[zp(-step), lo:hi]
            arrive(ref, z_sems.at[k, a, 0 if step == 1 else 1])
            send(ref, ref, z_sems.at[k, a, 2], dev(zh_=zp(step)))

    def z_rest(h, k, origin):
        if origin == 2:
            for a in range(2):
                lo, hi = cuts[a]
                arrive(h.at[zp(2), lo:hi], z_sems.at[k, a, 2])
        else:
            a, way = (1, 0) if origin == -1 else (0, 1)
            lo, hi = cuts[a]
            arrive(h.at[zp(origin), lo:hi], z_sems.at[k, a, way])

    origins = (0, -1, 1, 2)

    def s_start(s, k):
        ref = s.at[c, :, y]
        for d in (2, 1, 3):
            send(ref, ref, s_sems.at[k], dev(y_=yp(d)))

    def s_cross(s, k):
        arrive(s.at[c, :, 0 : Y - 1], s_sems.at[k])
        send(s.at[c], s.at[c], sc_sems.at[k], dev(c_=1 - c))

    z_start(h0, 0)
    for o in range(SURPLUS):
        send(parcels.at[o, 0:SHARE], arrived.at[o, 0:SHARE], head_sem, dev(x_=xp(o + 1)))
    loads[4].wait()
    for o in range(SURPLUS):
        for e in range(EXTRA):
            parcels[o, SHARE:ROWS, lanes(e)] = scaled(OWN + EXTRA * (o + 1) + e, SHARE, ROWS)
        send(parcels.at[o, SHARE:ROWS], arrived.at[o, SHARE:ROWS], body_sem, dev(x_=xp(o + 1)))

    def with_parcels(first, last):
        mine = [scaled(OWN + e, first, last) for e in range(EXTRA)]
        total = jnp.concatenate(mine, axis=1)
        for o in range(SURPLUS):
            total = total + arrived[o, first:last, :]
        return total

    arrive(arrived.at[:, 0:SHARE], head_sem)
    h1[zh] = with_parcels(0, SHARE)
    z_start(h1, 1)
    for k in range(OWN):
        for half in range(2):
            s0[c, half, y, :, lanes(k)] = scaled(k, half * HALF, (half + 1) * HALF)
    s_start(s0, 0)

    def token(step, sem):
        first, last = (0, ZL - 1) if step == 1 else (ZL - 1, 0)

        @pl.when(zl != first)
        def _():
            pl.semaphore_wait(sem, 1)

        @pl.when(zl != last)
        def _():
            target = dev(zl_=zl + step)
            pl.semaphore_signal(sem, inc=1, device_id=target, device_id_type=mesh_id)

    @pl.when(zl < ZL // 2)
    def _():
        token(1, below_sem)
        token(-1, above_sem)

    @pl.when(zl >= ZL // 2)
    def _():
        token(-1, above_sem)
        token(1, below_sem)

    group_of = {0: slice(*GROUPS[0]), 1: slice(*GROUPS[1])}

    def product(g):
        first, last = GROUPS[g]
        at = [zp(origins[n]) for n in range(first, last)]
        a = jnp.concatenate([h0[z] for z in at], axis=0)
        b = jnp.concatenate([h1[z] for z in at], axis=0)
        block = nt_dot(a, s0[...].reshape(HELD, W0)) + nt_dot(b, s1[...].reshape(HELD, W1))
        block = block.astype(BF16)
        wide = HELD // X
        for n in range(first, last):
            for t in range(X):
                rows = slice((n - first) * SHARE, (n - first + 1) * SHARE)
                part[n, t] = block[rows, t * wide : (t + 1) * wide]
        for d in (2, 1, 3):
            send(part.at[group_of[g], xp(d)], xin.at[group_of[g], x], xr_sems.at[g], dev(x_=xp(d)))
        copy = pltpu.make_async_copy(part.at[group_of[g], x], xin.at[group_of[g], x], xr_sems.at[g])
        copy.start()

    def x_reduce(g):
        arrive(xin.at[group_of[g]], xr_sems.at[g])
        for n in range(*GROUPS[g]):
            total = xin[n, 0].astype(F32)
            for s in range(1, X):
                total = total + xin[n, s].astype(F32)
            total = total.astype(BF16)
            for j in range(Y):
                xsum[n, j] = total[:, j * HALF : (j + 1) * HALF]
        for j in range(Y):
            here = zl == OWNER_OF[j]
            src, dst = xsum.at[group_of[g], j], zin.at[group_of[g], zl]
            send(src, dst, zr_sems.at[g], dev(zl_=OWNER_OF[j]), jnp.logical_not(here))
            keep(src, dst, zr_sems.at[g], here)

    owner = jnp.logical_and(zl >= min(OWNER_OF), zl <= max(OWNER_OF))
    seat = jnp.where(zl == OWNER_OF[0], 0, jnp.where(zl == OWNER_OF[1], 1, jnp.where(zl == OWNER_OF[2], 2, 3)))
    gives = jnp.logical_and(owner, seat < ZL // ZH)
    goes_to = (seat * ZH + zh) % ZL

    def z_reduce(g):
        @pl.when(owner)
        def _():
            arrive(zin.at[group_of[g]], zr_sems.at[g])
            for n in range(*GROUPS[g]):
                total = zin[n, 0].astype(F32)
                for s in range(1, ZL):
                    total = total + zin[n, s].astype(F32)
                own[n] = total.astype(BF16)

        src = own.at[group_of[g]]
        for d in (2, 1, 3):
            send(src, trail.at[group_of[g], y, c], tz_sems.at[g], dev(zl_=goes_to, zh_=zp(d)), gives)
        for d in range(1, ZL):
            send(src, zg.at[group_of[g], seat], zg_sems.at[g], dev(zl_=(zl + d) % ZL), owner)
        keep(src, zg.at[group_of[g], seat], zg_sems.at[g], owner)

    def gather(g):
        arrive(zg.at[group_of[g]], zg_sems.at[g])
        keep(zg.at[group_of[g], zl // ZH], trail.at[group_of[g], y, c], tz_sems.at[g], zh == zl % ZH)
        side = pl.ds(pl.multiple_of((x % 2) * HALF, HALF), HALF)
        dst = full.at[group_of[g], y * CORES + c, :, side]
        for j in range(Y):
            src = zg.at[group_of[g], j]
            for d in range(X):
                target = dev(x_=xp(d), y_=j, c_=x // 2)
                if d:
                    send(src, dst, xg_sems.at[g], target)
                else:
                    here = jnp.logical_and(y == j, c == x // 2)
                    send(src, dst, xg_sems.at[g], target, jnp.logical_not(here))
                    keep(src, dst, xg_sems.at[g], here)

    def spread(g):
        ref = trail.at[group_of[g], y, c]
        arrive(ref, tz_sems.at[g])
        for d in (2, 1, 3):
            for cc in (c, 1 - c):
                send(ref, ref, ty_sems.at[g], dev(y_=yp(d), c_=cc))
        send(ref, ref, tc_sems.at[g], dev(c_=1 - c))

    def place(g):
        arrive(trail.at[group_of[g], 0 : Y - 1], ty_sems.at[g])
        arrive(trail.at[group_of[g], 0, 0], tc_sems.at[g])
        for n in range(*GROUPS[g]):
            natural[:, (zl % ZH + origins[n] + ZH) % ZH] = trail[n]

    def finish(g):
        arrive(full.at[group_of[g]], xg_sems.at[g])
        for n in range(*GROUPS[g]):
            step = tn_dot(full[n].reshape(SEG, ROWS), inv[zp(origins[n])].reshape(SEG, PANEL))
            if n == 0:
                acc[...] = step
            else:
                acc[...] += step

    def relay(h, k):
        z_relay(h, k)
        z_rest(h, k, -1)
        z_rest(h, k, 1)

    relay(h0, 0)
    arrive(arrived.at[:, SHARE:ROWS], body_sem)
    for half in range(2):
        s1[c, half, y] = with_parcels(half * HALF, (half + 1) * HALF)
    s_start(s1, 1)
    relay(h1, 1)
    s_cross(s0, 0)
    s_cross(s1, 1)
    for s, k in ((s0, 0), (s1, 1)):
        arrive(s.at[1 - c], sc_sems.at[k])
    product(0)
    for h, k in heads:
        z_rest(h, k, 2)
    product(1)
    x_reduce(0)
    x_reduce(1)
    z_reduce(0)
    z_reduce(1)
    for copy in inv_copies:
        copy.wait()
    gather(0)
    gather(1)
    spread(0)
    finish(0)
    place(0)
    finish(1)
    finished = acc[...].astype(BF16)
    spread(1)
    place(1)
    loads[5].wait()
    update = jnp.dot(finished, natural[...].reshape(PANEL, HALF), preferred_element_type=F32)
    out[...] = slab[...] - update

    for pred, copy in pending:
        if pred is None:
            copy.wait_send()
        else:
            pl.when(pred)(copy.wait_send)


def body(border, col_index, barrier, counts, inverse, slab):
    dma = pltpu.SemaphoreType.DMA
    wide = HELD // X
    return pl.pallas_call(
        kernel,
        out_shape=jax.ShapeDtypeStruct(slab.shape, slab.dtype),
        in_specs=[pl.BlockSpec(memory_space=pl.ANY)] * 6,
        out_specs=pl.BlockSpec(memory_space=pltpu.VMEM),
        scratch_shapes=[
            pltpu.SMEM(counts.shape, counts.dtype),
            pltpu.VMEM(col_index.shape, col_index.dtype),
            pltpu.VMEM((barrier.shape[0] // BW, BW), barrier.dtype),
            pltpu.VMEM(border.shape, border.dtype),
            pltpu.VMEM(slab.shape, slab.dtype),
            pltpu.VMEM((SURPLUS, ROWS, W1), BF16),
            pltpu.VMEM((SURPLUS, ROWS, W1), BF16),
            pltpu.VMEM((CORES, 2, Y, HALF, W0), BF16),
            pltpu.VMEM((CORES, 2, Y, HALF, W1), BF16),
            pltpu.VMEM((ZH, SHARE, W0), BF16),
            pltpu.VMEM((ZH, SHARE, W1), BF16),
            pltpu.VMEM((ZH, X, SHARE, wide), BF16),
            pltpu.VMEM((ZH, X, SHARE, wide), BF16),
            pltpu.VMEM((ZH, Y, SHARE, HALF), BF16),
            pltpu.VMEM((ZH, ZL, SHARE, HALF), BF16),
            pltpu.VMEM((ZH, SHARE, HALF), BF16),
            pltpu.VMEM((ZH, Y, SHARE, HALF), BF16),
            pltpu.VMEM((ZH, Y * CORES, SHARE, ROWS), BF16),
            pltpu.VMEM((ZH, Y, CORES, SHARE, HALF), BF16),
            pltpu.VMEM((Y, ZH, CORES, SHARE, HALF), BF16),
            pltpu.VMEM((ZH, Y, CORES * SHARE, PANEL), BF16),
            pltpu.VMEM((ROWS, PANEL), F32),
            dma((128,)), dma((6,)), dma((ZH,)), dma, dma, dma((2,)), dma((2,)), dma((2, 2, 3)),
            dma((2,)), dma((2,)), dma((2,)), dma((2,)), dma((2,)), dma((2,)), dma((2,)),
            pltpu.SemaphoreType.REGULAR, pltpu.SemaphoreType.REGULAR,
        ],
        compiler_params=pltpu.CompilerParams(
            collective_id=0, has_side_effects=True, vmem_limit_bytes=67043328
        ),
        name="panel_update",
    )(
        counts, col_index, barrier.reshape(-1, BW), border,
        inverse.reshape(Y, ZH, CORES * SHARE, PANEL), slab,
    )


def solution(mesh):
    return jax.shard_map(
        body,
        mesh=mesh,
        in_specs=(P("scen", "row", None), P("scen", None), P(), P(), P(), P("row", "scen")),
        out_specs=P("row", "scen"),
        check_vma=False,
    )
```

```python
import jax
import jax.numpy as jnp
from jax import lax
from jax.experimental import pallas as pl
from jax.experimental.pallas import tpu as pltpu
from jax.sharding import PartitionSpec as P

X, ZL, Y, ZH, CORES = 4, 8, 4, 4, 2
OWN, EXTRA, SURPLUS = 4, 3, 3
BW = 128
W0, W1 = OWN * BW, EXTRA * BW
ROWS, SHARE, PANEL, HALF = 256, 32, 1024, 128
SEG = PANEL // ZH
OWNER_OF = (3, 4, 2, 5)
GROUPS = ((0, 3), (3, 4))
F32, BF16 = jnp.float32, jnp.bfloat16


def tn_dot(a, b):
    return lax.dot_general(a, b, (((0,), (0,)), ((), ())), preferred_element_type=F32)


def kernel(
    counts_in, index_in, table_in, border_in, inverse, slab_in, out,
    counts, index, table, border, slab, parcels, arrived, s0, s1, h0, h1,
    part, xin, xsum, zin, own, zg, full, trail, natural, inv, acc,
    send_sems, in_sems, inv_sem, head_sem, body_sem, s_sems, y_sems, z_sems,
    xr_sems, zr_sems, zg_sems, xg_sems, tz_sems, tc_sems, below_sem, above_sem,
):
    sc, rw = lax.axis_index("scen"), lax.axis_index("row")
    x, zl = sc % X, sc // X
    y, zh, c = rw // (ZH * CORES), (rw // CORES) % ZH, rw % CORES
    mesh_id = pl.DeviceIdType.MESH

    def dev(x_=x, zl_=zl, y_=y, zh_=zh, c_=c):
        return (zl_ * X + x_, (y_ * ZH + zh_) * CORES + c_)

    def xp(d):
        return (x + d) % X

    def yp(d):
        return (y + d) % Y

    def zp(d):
        return (zh + d + ZH) % ZH

    pending = []

    def send(src, dst, sem, target, pred=None):
        copy = pltpu.make_async_remote_copy(
            src_ref=src, dst_ref=dst, send_sem=send_sems.at[len(pending)], recv_sem=sem,
            device_id=target, device_id_type=mesh_id,
        )
        pending.append((pred, copy))
        if pred is None:
            copy.start()
        else:
            pl.when(pred)(copy.start)

    def keep(src, dst, sem, pred):
        copy = pltpu.make_async_copy(src, dst, sem)
        pl.when(pred)(copy.start)

    def arrive(ref, sem):
        pltpu.make_async_copy(ref, ref, sem).wait()

    loads = [
        pltpu.make_async_copy(source, target, in_sems.at[n])
        for n, (source, target) in enumerate((
            (index_in, index), (table_in, table), (counts_in, counts),
            (border_in.at[:, 0:SHARE], border.at[:, 0:SHARE]),
            (border_in.at[:, SHARE:ROWS], border.at[:, SHARE:ROWS]),
            (slab_in, slab),
        ))
    ]
    for copy in loads:
        copy.start()

    barrier = pltpu.get_barrier_semaphore()
    peers = [dev(x_=xp(d)) for d in range(1, X)] + [dev(y_=yp(d)) for d in range(1, Y)]
    peers += [dev(c_=1 - c), dev(zh_=zp(1)), dev(zh_=zp(-1))]
    for peer in peers:
        pl.semaphore_signal(barrier, inc=1, device_id=peer, device_id_type=mesh_id)
    up, down = zl < ZL - 1, zl > 0
    for pred, step in ((up, 1), (down, -1)):
        @pl.when(pred)
        def _(step=step):
            target = dev(zl_=zl + step)
            pl.semaphore_signal(barrier, inc=1, device_id=target, device_id_type=mesh_id)

    inv_copies = [
        pltpu.make_async_copy(inverse.at[:, b], inv.at[b], inv_sem.at[b]) for b in range(ZH)
    ]
    for copy in inv_copies:
        copy.start()

    for copy in loads[0:3]:
        copy.wait()
    indices = index[...]
    high, low = indices // BW, indices % BW
    weights = jnp.zeros(indices.shape, F32)
    for h in range(table.shape[0]):
        row = jnp.broadcast_to(table[h : h + 1, :], indices.shape)
        picked = jnp.take_along_axis(row, low, axis=1, mode="promise_in_bounds")
        weights = jnp.where(high == h, picked, weights)
    slots = lax.broadcasted_iota(jnp.int32, indices.shape, 0)
    weights = jnp.where(slots < counts[sc], weights, 0.0)

    def scaled(k, first, last):
        rows = border[k, first:last, :].astype(F32)
        return (rows * weights[k : k + 1, :]).astype(BF16)

    def lanes(k):
        return slice(k * BW, (k + 1) * BW)

    loads[3].wait()
    for k in range(OWN):
        h0[zh, y, :, lanes(k)] = scaled(k, 0, SHARE)
    for o in range(SURPLUS):
        for e in range(EXTRA):
            parcels[o, 0:SHARE, lanes(e)] = scaled(OWN + EXTRA * (o + 1) + e, 0, SHARE)
    loads[4].wait()
    for k in range(OWN):
        for half in range(2):
            s0[c, half, lanes(k), :] = scaled(k, half * HALF, (half + 1) * HALF).T
    for o in range(SURPLUS):
        for e in range(EXTRA):
            parcels[o, SHARE:ROWS, lanes(e)] = scaled(OWN + EXTRA * (o + 1) + e, SHARE, ROWS)
    near = up.astype(jnp.int32) + down.astype(jnp.int32)
    pl.semaphore_wait(barrier, len(peers) + near)

    heads = ((h0, 0), (h1, 1))
    cuts = ((0, SHARE // 2), (SHARE // 2, SHARE))

    def z_start(h, k):
        for a, step in ((0, 1), (1, -1), (1, 1), (0, -1)):
            lo, hi = cuts[a]
            ref = h.at[zh, y, lo:hi]
            send(ref, ref, z_sems.at[k, a, 0 if step == 1 else 1], dev(zh_=zp(step)))

    def z_relay(h, k):
        for a, step in ((0, 1), (1, -1)):
            lo, hi = cuts[a]
            ref = h.at[zp(-step), y, lo:hi]
            arrive(ref, z_sems.at[k, a, 0 if step == 1 else 1])
            send(ref, ref, z_sems.at[k, a, 2], dev(zh_=zp(step)))

    def z_rest(h, k, origin):
        if origin == 2:
            for a in range(2):
                lo, hi = cuts[a]
                arrive(h.at[zp(2), y, lo:hi], z_sems.at[k, a, 2])
        else:
            a, way = (1, 0) if origin == -1 else (0, 1)
            lo, hi = cuts[a]
            arrive(h.at[zp(origin), y, lo:hi], z_sems.at[k, a, way])

    origins = (0, -1, 1, 2)

    def y_start(h, k, n):
        ref = h.at[zp(origins[n]), y]
        for d in (2, 1, 3):
            send(ref, ref, y_sems.at[k, n], dev(y_=yp(d)))

    def y_rest(n):
        for h, k in heads:
            arrive(h.at[zp(origins[n]), 0 : Y - 1], y_sems.at[k, n])

    def s_cross(s, k):
        send(s.at[c], s.at[c], s_sems.at[k], dev(c_=1 - c))

    def token(seat_on_line):
        for at, step, sem in ((seat_on_line, 1, below_sem), (ZL - 1 - seat_on_line, -1, above_sem)):
            @pl.when(zl == at)
            def _(step=step, sem=sem):
                if seat_on_line > 0:
                    pl.semaphore_wait(sem, 1)
                if seat_on_line < ZL - 1:
                    target = dev(zl_=zl + step)
                    pl.semaphore_signal(sem, inc=1, device_id=target, device_id_type=mesh_id)

    token(0)
    z_start(h0, 0)
    for o in range(SURPLUS):
        send(parcels.at[o, 0:SHARE], arrived.at[o, 0:SHARE], head_sem, dev(x_=xp(o + 1)))
    y_start(h0, 0, 0)
    s_cross(s0, 0)
    for o in range(SURPLUS):
        send(parcels.at[o, SHARE:ROWS], arrived.at[o, SHARE:ROWS], body_sem, dev(x_=xp(o + 1)))
    token(1)
    token(2)

    def with_parcels(first, last):
        mine = [scaled(OWN + e, first, last) for e in range(EXTRA)]
        total = jnp.concatenate(mine, axis=1)
        for o in range(SURPLUS):
            total = total + arrived[o, first:last, :]
        return total

    arrive(arrived.at[:, 0:SHARE], head_sem)
    h1[zh, y] = with_parcels(0, SHARE)
    z_start(h1, 1)
    y_start(h1, 1, 0)
    token(3)
    token(4)

    group_of = {0: slice(*GROUPS[0]), 1: slice(*GROUPS[1])}

    def product(g):
        first, last = GROUPS[g]
        at = [zp(origins[n]) for n in range(first, last)]
        a = jnp.concatenate([h0[z].reshape(BW, W0) for z in at], axis=0)
        b = jnp.concatenate([h1[z].reshape(BW, W1) for z in at], axis=0)
        for t in range(X):
            block = jnp.dot(a, s0[t // 2, t % 2], preferred_element_type=F32)
            block = block + jnp.dot(b, s1[t // 2, t % 2], preferred_element_type=F32)
            block = block.astype(BF16).reshape(last - first, Y, SHARE, HALF)
            for n in range(first, last):
                part[n, t] = block[n - first]
        for d in (2, 1, 3):
            send(part.at[group_of[g], xp(d)], xin.at[group_of[g], x], xr_sems.at[g], dev(x_=xp(d)))
        copy = pltpu.make_async_copy(part.at[group_of[g], x], xin.at[group_of[g], x], xr_sems.at[g])
        copy.start()

    def x_reduce(g):
        arrive(xin.at[group_of[g]], xr_sems.at[g])
        for n in range(*GROUPS[g]):
            total = xin[n, 0].astype(F32)
            for s in range(1, X):
                total = total + xin[n, s].astype(F32)
            xsum[n] = total.astype(BF16)
        for j in range(Y):
            here = zl == OWNER_OF[j]
            src, dst = xsum.at[group_of[g], j], zin.at[group_of[g], zl]
            send(src, dst, zr_sems.at[g], dev(zl_=OWNER_OF[j]), jnp.logical_not(here))
            keep(src, dst, zr_sems.at[g], here)

    owner = jnp.logical_and(zl >= min(OWNER_OF), zl <= max(OWNER_OF))
    seat = jnp.where(zl == OWNER_OF[0], 0, jnp.where(zl == OWNER_OF[1], 1, jnp.where(zl == OWNER_OF[2], 2, 3)))
    gives = jnp.logical_and(owner, y < ZL // ZH)
    goes_to = (y * ZH + zh) % ZL
    on_line = y == zl // ZH

    def z_reduce(g):
        @pl.when(owner)
        def _():
            arrive(zin.at[group_of[g]], zr_sems.at[g])
            for n in range(*GROUPS[g]):
                total = zin[n, 0].astype(F32)
                for s in range(1, ZL):
                    total = total + zin[n, s].astype(F32)
                own[n] = total.astype(BF16)

        src = own.at[group_of[g]]
        for d in (2, 1, 3):
            send(src, trail.at[group_of[g], seat, c], tz_sems.at[g], dev(zl_=goes_to, zh_=zp(d)), gives)
        for d in range(1, ZL):
            send(src, zg.at[group_of[g], seat], zg_sems.at[g], dev(zl_=(zl + d) % ZL), owner)
        keep(src, zg.at[group_of[g], seat], zg_sems.at[g], owner)

    def gather(g):
        arrive(zg.at[group_of[g]], zg_sems.at[g])
        src = zg.at[group_of[g]]
        source = jnp.logical_and(on_line, zh == zl % ZH)
        keep(src, trail.at[group_of[g], :, c], tz_sems.at[g], source)
        side = pl.ds(pl.multiple_of((x % 2) * HALF, HALF), HALF)
        dst = full.at[group_of[g], :, c, :, side]
        for d in (2, 1, 3):
            send(src, dst, xg_sems.at[g], dev(x_=xp(d), c_=x // 2))
        send(src, dst, xg_sems.at[g], dev(c_=1 - c), c != x // 2)
        keep(src, dst, xg_sems.at[g], c == x // 2)

    def spread(g):
        ref = trail.at[group_of[g], :, c]
        arrive(ref, tz_sems.at[g])
        for d in (2, 1, 3):
            send(ref, ref, tz_sems.at[g], dev(y_=yp(d)), on_line)
        send(ref, ref, tc_sems.at[g], dev(c_=1 - c))

    def place(g):
        arrive(trail.at[group_of[g], :, 1 - c], tc_sems.at[g])
        for n in range(*GROUPS[g]):
            natural[:, (zl % ZH + origins[n] + ZH) % ZH] = trail[n]

    def finish(g):
        arrive(full.at[group_of[g]], xg_sems.at[g])
        for n in range(*GROUPS[g]):
            step = tn_dot(full[n].reshape(SEG, ROWS), inv[zp(origins[n])].reshape(SEG, PANEL))
            if n == 0:
                acc[...] = step
            else:
                acc[...] += step

    arrive(arrived.at[:, SHARE:ROWS], body_sem)
    for half in range(2):
        extra = with_parcels(half * HALF, (half + 1) * HALF)
        for e in range(EXTRA):
            s1[c, half, lanes(e), :] = extra[:, lanes(e)].T
    s_cross(s1, 1)
    for place_on_line in range(5, ZL):
        token(place_on_line)
    for h, k in heads:
        z_relay(h, k)
        for n in (1, 2):
            z_rest(h, k, origins[n])
            y_start(h, k, n)
    for s, k in ((s0, 0), (s1, 1)):
        arrive(s.at[1 - c], s_sems.at[k])
    for n in range(3):
        y_rest(n)
    product(0)
    for h, k in heads:
        z_rest(h, k, 2)
        y_start(h, k, 3)
    x_reduce(0)
    y_rest(3)
    product(1)
    x_reduce(1)
    z_reduce(0)
    z_reduce(1)
    for copy in inv_copies:
        copy.wait()
    gather(0)
    gather(1)
    finish(0)
    finish(1)
    finished = acc[...].astype(BF16)
    spread(0)
    place(0)
    spread(1)
    place(1)
    loads[5].wait()
    update = jnp.dot(finished, natural[...].reshape(PANEL, HALF), preferred_element_type=F32)
    out[...] = slab[...] - update

    for pred, copy in pending:
        if pred is None:
            copy.wait_send()
        else:
            pl.when(pred)(copy.wait_send)


def body(border, col_index, barrier, counts, inverse, slab):
    dma = pltpu.SemaphoreType.DMA
    return pl.pallas_call(
        kernel,
        out_shape=jax.ShapeDtypeStruct(slab.shape, slab.dtype),
        in_specs=[pl.BlockSpec(memory_space=pl.ANY)] * 6,
        out_specs=pl.BlockSpec(memory_space=pltpu.VMEM),
        scratch_shapes=[
            pltpu.SMEM(counts.shape, counts.dtype),
            pltpu.VMEM(col_index.shape, col_index.dtype),
            pltpu.VMEM((barrier.shape[0] // BW, BW), barrier.dtype),
            pltpu.VMEM(border.shape, border.dtype),
            pltpu.VMEM(slab.shape, slab.dtype),
            pltpu.VMEM((SURPLUS, ROWS, W1), BF16),
            pltpu.VMEM((SURPLUS, ROWS, W1), BF16),
            pltpu.VMEM((CORES, 2, W0, HALF), BF16),
            pltpu.VMEM((CORES, 2, W1, HALF), BF16),
            pltpu.VMEM((ZH, Y, SHARE, W0), BF16),
            pltpu.VMEM((ZH, Y, SHARE, W1), BF16),
            pltpu.VMEM((ZH, X, Y, SHARE, HALF), BF16),
            pltpu.VMEM((ZH, X, Y, SHARE, HALF), BF16),
            pltpu.VMEM((ZH, Y, SHARE, HALF), BF16),
            pltpu.VMEM((ZH, ZL, SHARE, HALF), BF16),
            pltpu.VMEM((ZH, SHARE, HALF), BF16),
            pltpu.VMEM((ZH, Y, SHARE, HALF), BF16),
            pltpu.VMEM((ZH, Y, CORES, SHARE, ROWS), BF16),
            pltpu.VMEM((ZH, Y, CORES, SHARE, HALF), BF16),
            pltpu.VMEM((Y, ZH, CORES, SHARE, HALF), BF16),
            pltpu.VMEM((ZH, Y, CORES * SHARE, PANEL), BF16),
            pltpu.VMEM((ROWS, PANEL), F32),
            dma((128,)), dma((6,)), dma((ZH,)), dma, dma, dma((2,)), dma((2, 4)), dma((2, 2, 3)),
            dma((2,)), dma((2,)), dma((2,)), dma((2,)), dma((2,)), dma((2,)),
            pltpu.SemaphoreType.REGULAR, pltpu.SemaphoreType.REGULAR,
        ],
        compiler_params=pltpu.CompilerParams(
            collective_id=0, has_side_effects=True, vmem_limit_bytes=67043328
        ),
        name="panel_update",
    )(
        counts, col_index, barrier.reshape(-1, BW), border,
        inverse.reshape(Y, ZH, CORES * SHARE, PANEL), slab,
    )


def solution(mesh):
    return jax.shard_map(
        body,
        mesh=mesh,
        in_specs=(P("scen", "row", None), P("scen", None), P(), P(), P(), P("row", "scen")),
        out_specs=P("row", "scen"),
        check_vma=False,
    )
```

```python
import jax
import jax.numpy as jnp
from jax import lax
from jax.experimental import pallas as pl
from jax.experimental.pallas import tpu as pltpu
from jax.sharding import PartitionSpec as P

X, ZL, Y, ZH, CORES = 4, 8, 4, 4, 2
OWN, EXTRA, SURPLUS = 4, 3, 3
BW = 128
W0, W1 = OWN * BW, EXTRA * BW
ROWS, SHARE, PANEL, HALF = 256, 32, 1024, 128
SEG = PANEL // ZH
OWNER_OF = (3, 4, 2, 5)
GROUPS = ((0, 1), (1, 3), (3, 4))
F32, BF16 = jnp.float32, jnp.bfloat16


def tn_dot(a, b):
    return lax.dot_general(a, b, (((0,), (0,)), ((), ())), preferred_element_type=F32)


def kernel(
    counts_in, index_in, table_in, border_in, inverse, slab_in, out,
    counts, index, table, border, slab, parcels, arrived, s0, s1, h0, h1,
    part, xin, xsum, zin, own, zg, full, trail, natural, inv, acc,
    send_sems, in_sems, inv_sem, head_sem, body_sem, s_sems, y_sems, z_sems,
    xr_sems, zr_sems, zg_sems, xg_sems, tz_sems, tc_sems, below_sem, above_sem,
):
    sc, rw = lax.axis_index("scen"), lax.axis_index("row")
    x, zl = sc % X, sc // X
    y, zh, c = rw // (ZH * CORES), (rw // CORES) % ZH, rw % CORES
    mesh_id = pl.DeviceIdType.MESH

    def dev(x_=x, zl_=zl, y_=y, zh_=zh, c_=c):
        return (zl_ * X + x_, (y_ * ZH + zh_) * CORES + c_)

    def xp(d):
        return (x + d) % X

    def yp(d):
        return (y + d) % Y

    def zp(d):
        return (zh + d + ZH) % ZH

    pending = []

    def send(src, dst, sem, target, pred=None):
        copy = pltpu.make_async_remote_copy(
            src_ref=src, dst_ref=dst, send_sem=send_sems.at[len(pending)], recv_sem=sem,
            device_id=target, device_id_type=mesh_id,
        )
        pending.append((pred, copy))
        if pred is None:
            copy.start()
        else:
            pl.when(pred)(copy.start)

    def keep(src, dst, sem, pred):
        copy = pltpu.make_async_copy(src, dst, sem)
        pl.when(pred)(copy.start)

    def arrive(ref, sem):
        pltpu.make_async_copy(ref, ref, sem).wait()

    loads = [
        pltpu.make_async_copy(source, target, in_sems.at[n])
        for n, (source, target) in enumerate((
            (index_in, index), (table_in, table), (counts_in, counts),
            (border_in.at[:, 0:SHARE], border.at[:, 0:SHARE]),
            (border_in.at[:, SHARE:ROWS], border.at[:, SHARE:ROWS]),
            (slab_in, slab),
        ))
    ]
    for copy in loads:
        copy.start()

    barrier = pltpu.get_barrier_semaphore()
    peers = [dev(x_=xp(d)) for d in range(1, X)] + [dev(y_=yp(d)) for d in range(1, Y)]
    peers += [dev(c_=1 - c), dev(zh_=zp(1)), dev(zh_=zp(-1))]
    for peer in peers:
        pl.semaphore_signal(barrier, inc=1, device_id=peer, device_id_type=mesh_id)
    up, down = zl < ZL - 1, zl > 0
    for pred, step in ((up, 1), (down, -1)):
        @pl.when(pred)
        def _(step=step):
            target = dev(zl_=zl + step)
            pl.semaphore_signal(barrier, inc=1, device_id=target, device_id_type=mesh_id)

    inv_copies = [
        pltpu.make_async_copy(inverse.at[:, b], inv.at[b], inv_sem.at[b]) for b in range(ZH)
    ]
    for copy in inv_copies:
        copy.start()

    for copy in loads[0:3]:
        copy.wait()
    indices = index[...]
    high, low = indices // BW, indices % BW
    weights = jnp.zeros(indices.shape, F32)
    for h in range(table.shape[0]):
        row = jnp.broadcast_to(table[h : h + 1, :], indices.shape)
        picked = jnp.take_along_axis(row, low, axis=1, mode="promise_in_bounds")
        weights = jnp.where(high == h, picked, weights)
    slots = lax.broadcasted_iota(jnp.int32, indices.shape, 0)
    weights = jnp.where(slots < counts[sc], weights, 0.0)

    def scaled(k, first, last):
        rows = border[k, first:last, :].astype(F32)
        return (rows * weights[k : k + 1, :]).astype(BF16)

    def lanes(k):
        return slice(k * BW, (k + 1) * BW)

    loads[3].wait()
    for k in range(OWN):
        h0[zh, y, :, lanes(k)] = scaled(k, 0, SHARE)
    for o in range(SURPLUS):
        for e in range(EXTRA):
            parcels[o, 0:SHARE, lanes(e)] = scaled(OWN + EXTRA * (o + 1) + e, 0, SHARE)
    loads[4].wait()
    for k in range(OWN):
        for half in range(2):
            s0[c, half, lanes(k), :] = scaled(k, half * HALF, (half + 1) * HALF).T
    for o in range(SURPLUS):
        for e in range(EXTRA):
            parcels[o, SHARE:ROWS, lanes(e)] = scaled(OWN + EXTRA * (o + 1) + e, SHARE, ROWS)
    near = up.astype(jnp.int32) + down.astype(jnp.int32)
    pl.semaphore_wait(barrier, len(peers) + near)

    heads = ((h0, 0), (h1, 1))
    cuts = ((0, SHARE // 2), (SHARE // 2, SHARE))

    def z_start(h, k):
        for a, step in ((0, 1), (1, -1), (1, 1), (0, -1)):
            lo, hi = cuts[a]
            ref = h.at[zh, y, lo:hi]
            send(ref, ref, z_sems.at[k, a, 0 if step == 1 else 1], dev(zh_=zp(step)))

    def z_relay(h, k):
        for a, step in ((0, 1), (1, -1)):
            lo, hi = cuts[a]
            ref = h.at[zp(-step), y, lo:hi]
            arrive(ref, z_sems.at[k, a, 0 if step == 1 else 1])
            send(ref, ref, z_sems.at[k, a, 2], dev(zh_=zp(step)))

    def z_rest(h, k, origin):
        if origin == 2:
            for a in range(2):
                lo, hi = cuts[a]
                arrive(h.at[zp(2), y, lo:hi], z_sems.at[k, a, 2])
        else:
            a, way = (1, 0) if origin == -1 else (0, 1)
            lo, hi = cuts[a]
            arrive(h.at[zp(origin), y, lo:hi], z_sems.at[k, a, way])

    origins = (0, -1, 1, 2)

    def y_start(h, k, n):
        ref = h.at[zp(origins[n]), y]
        for d in (2, 1, 3):
            send(ref, ref, y_sems.at[k, n], dev(y_=yp(d)))

    def y_rest(n):
        for h, k in heads:
            arrive(h.at[zp(origins[n]), 0 : Y - 1], y_sems.at[k, n])

    def s_cross(s, k):
        send(s.at[c], s.at[c], s_sems.at[k], dev(c_=1 - c))

    def token(seat_on_line):
        for at, step, sem in ((seat_on_line, 1, below_sem), (ZL - 1 - seat_on_line, -1, above_sem)):
            @pl.when(zl == at)
            def _(step=step, sem=sem):
                if seat_on_line > 0:
                    pl.semaphore_wait(sem, 1)
                if seat_on_line < ZL - 1:
                    target = dev(zl_=zl + step)
                    pl.semaphore_signal(sem, inc=1, device_id=target, device_id_type=mesh_id)

    token(0)
    z_start(h0, 0)
    for o in range(SURPLUS):
        send(parcels.at[o, 0:SHARE], arrived.at[o, 0:SHARE], head_sem, dev(x_=xp(o + 1)))
    y_start(h0, 0, 0)
    s_cross(s0, 0)
    for o in range(SURPLUS):
        send(parcels.at[o, SHARE:ROWS], arrived.at[o, SHARE:ROWS], body_sem, dev(x_=xp(o + 1)))
    token(1)
    token(2)

    def with_parcels(first, last):
        mine = [scaled(OWN + e, first, last) for e in range(EXTRA)]
        total = jnp.concatenate(mine, axis=1)
        for o in range(SURPLUS):
            total = total + arrived[o, first:last, :]
        return total

    arrive(arrived.at[:, 0:SHARE], head_sem)
    h1[zh, y] = with_parcels(0, SHARE)
    z_start(h1, 1)
    y_start(h1, 1, 0)
    token(3)
    token(4)

    group_of = [slice(*group) for group in GROUPS]

    def product(g):
        first, last = GROUPS[g]
        at = [zp(origins[n]) for n in range(first, last)]
        a = jnp.concatenate([h0[z].reshape(BW, W0) for z in at], axis=0)
        b = jnp.concatenate([h1[z].reshape(BW, W1) for z in at], axis=0)
        for t in range(X):
            block = jnp.dot(a, s0[t // 2, t % 2], preferred_element_type=F32)
            block = block + jnp.dot(b, s1[t // 2, t % 2], preferred_element_type=F32)
            block = block.astype(BF16).reshape(last - first, Y, SHARE, HALF)
            for n in range(first, last):
                part[n, t] = block[n - first]
        for d in (2, 1, 3):
            send(part.at[group_of[g], xp(d)], xin.at[group_of[g], x], xr_sems.at[g], dev(x_=xp(d)))
        copy = pltpu.make_async_copy(part.at[group_of[g], x], xin.at[group_of[g], x], xr_sems.at[g])
        copy.start()

    def x_reduce(g):
        arrive(xin.at[group_of[g]], xr_sems.at[g])
        for n in range(*GROUPS[g]):
            total = xin[n, 0].astype(F32)
            for s in range(1, X):
                total = total + xin[n, s].astype(F32)
            xsum[n] = total.astype(BF16)
        for j in range(Y):
            here = zl == OWNER_OF[j]
            src, dst = xsum.at[group_of[g], j], zin.at[group_of[g], zl]
            send(src, dst, zr_sems.at[g], dev(zl_=OWNER_OF[j]), jnp.logical_not(here))
            keep(src, dst, zr_sems.at[g], here)

    owner = jnp.logical_and(zl >= min(OWNER_OF), zl <= max(OWNER_OF))
    seat = jnp.where(zl == OWNER_OF[0], 0, jnp.where(zl == OWNER_OF[1], 1, jnp.where(zl == OWNER_OF[2], 2, 3)))
    gives = jnp.logical_and(owner, y < ZL // ZH)
    goes_to = (y * ZH + zh) % ZL
    on_line = y == zl // ZH

    def z_reduce(g):
        @pl.when(owner)
        def _():
            arrive(zin.at[group_of[g]], zr_sems.at[g])
            for n in range(*GROUPS[g]):
                total = zin[n, 0].astype(F32)
                for s in range(1, ZL):
                    total = total + zin[n, s].astype(F32)
                own[n] = total.astype(BF16)

        src = own.at[group_of[g]]
        for d in (2, 1, 3):
            send(src, trail.at[group_of[g], seat, c], tz_sems.at[g], dev(zl_=goes_to, zh_=zp(d)), gives)
        for d in range(1, ZL):
            send(src, zg.at[group_of[g], seat], zg_sems.at[g], dev(zl_=(zl + d) % ZL), owner)
        keep(src, zg.at[group_of[g], seat], zg_sems.at[g], owner)

    def gather(g):
        arrive(zg.at[group_of[g]], zg_sems.at[g])
        src = zg.at[group_of[g]]
        source = jnp.logical_and(on_line, zh == zl % ZH)
        keep(src, trail.at[group_of[g], :, c], tz_sems.at[g], source)
        side = pl.ds(pl.multiple_of((x % 2) * HALF, HALF), HALF)
        dst = full.at[group_of[g], :, c, :, side]
        for d in (2, 1, 3):
            send(src, dst, xg_sems.at[g], dev(x_=xp(d), c_=x // 2))
        send(src, dst, xg_sems.at[g], dev(c_=1 - c), c != x // 2)
        keep(src, dst, xg_sems.at[g], c == x // 2)

    def spread(g):
        ref = trail.at[group_of[g], :, c]
        arrive(ref, tz_sems.at[g])
        for d in (2, 1, 3):
            send(ref, ref, tz_sems.at[g], dev(y_=yp(d)), on_line)
        send(ref, ref, tc_sems.at[g], dev(c_=1 - c))

    def place(g):
        arrive(trail.at[group_of[g], :, 1 - c], tc_sems.at[g])
        for n in range(*GROUPS[g]):
            natural[:, (zl % ZH + origins[n] + ZH) % ZH] = trail[n]

    def finish(g):
        arrive(full.at[group_of[g]], xg_sems.at[g])
        for n in range(*GROUPS[g]):
            step = tn_dot(full[n].reshape(SEG, ROWS), inv[zp(origins[n])].reshape(SEG, PANEL))
            if n == 0:
                acc[...] = step
            else:
                acc[...] += step

    arrive(arrived.at[:, SHARE:ROWS], body_sem)
    for half in range(2):
        extra = with_parcels(half * HALF, (half + 1) * HALF)
        for e in range(EXTRA):
            s1[c, half, lanes(e), :] = extra[:, lanes(e)].T
    s_cross(s1, 1)
    for place_on_line in range(5, ZL):
        token(place_on_line)
    def relay(h, k):
        z_relay(h, k)
        for n in (1, 2):
            z_rest(h, k, origins[n])
            y_start(h, k, n)

    relay(h0, 0)
    for s, k in ((s0, 0), (s1, 1)):
        arrive(s.at[1 - c], s_sems.at[k])
    y_rest(0)
    product(0)
    relay(h1, 1)
    x_reduce(0)
    y_rest(1)
    y_rest(2)
    product(1)
    for h, k in heads:
        z_rest(h, k, 2)
        y_start(h, k, 3)
    z_reduce(0)
    y_rest(3)
    product(2)
    x_reduce(1)
    x_reduce(2)
    gather(0)
    z_reduce(1)
    z_reduce(2)
    for copy in inv_copies:
        copy.wait()
    finish(0)
    gather(1)
    gather(2)
    spread(0)
    finish(1)
    finish(2)
    finished = acc[...].astype(BF16)
    place(0)
    for g in (1, 2):
        spread(g)
    for g in (1, 2):
        place(g)
    loads[5].wait()
    update = jnp.dot(finished, natural[...].reshape(PANEL, HALF), preferred_element_type=F32)
    out[...] = slab[...] - update

    for pred, copy in pending:
        if pred is None:
            copy.wait_send()
        else:
            pl.when(pred)(copy.wait_send)


def body(border, col_index, barrier, counts, inverse, slab):
    dma = pltpu.SemaphoreType.DMA
    return pl.pallas_call(
        kernel,
        out_shape=jax.ShapeDtypeStruct(slab.shape, slab.dtype),
        in_specs=[pl.BlockSpec(memory_space=pl.ANY)] * 6,
        out_specs=pl.BlockSpec(memory_space=pltpu.VMEM),
        scratch_shapes=[
            pltpu.SMEM(counts.shape, counts.dtype),
            pltpu.VMEM(col_index.shape, col_index.dtype),
            pltpu.VMEM((barrier.shape[0] // BW, BW), barrier.dtype),
            pltpu.VMEM(border.shape, border.dtype),
            pltpu.VMEM(slab.shape, slab.dtype),
            pltpu.VMEM((SURPLUS, ROWS, W1), BF16),
            pltpu.VMEM((SURPLUS, ROWS, W1), BF16),
            pltpu.VMEM((CORES, 2, W0, HALF), BF16),
            pltpu.VMEM((CORES, 2, W1, HALF), BF16),
            pltpu.VMEM((ZH, Y, SHARE, W0), BF16),
            pltpu.VMEM((ZH, Y, SHARE, W1), BF16),
            pltpu.VMEM((ZH, X, Y, SHARE, HALF), BF16),
            pltpu.VMEM((ZH, X, Y, SHARE, HALF), BF16),
            pltpu.VMEM((ZH, Y, SHARE, HALF), BF16),
            pltpu.VMEM((ZH, ZL, SHARE, HALF), BF16),
            pltpu.VMEM((ZH, SHARE, HALF), BF16),
            pltpu.VMEM((ZH, Y, SHARE, HALF), BF16),
            pltpu.VMEM((ZH, Y, CORES, SHARE, ROWS), BF16),
            pltpu.VMEM((ZH, Y, CORES, SHARE, HALF), BF16),
            pltpu.VMEM((Y, ZH, CORES, SHARE, HALF), BF16),
            pltpu.VMEM((ZH, Y, CORES * SHARE, PANEL), BF16),
            pltpu.VMEM((ROWS, PANEL), F32),
            dma((128,)), dma((6,)), dma((ZH,)), dma, dma, dma((2,)), dma((2, 4)), dma((2, 2, 3)),
            dma((3,)), dma((3,)), dma((3,)), dma((3,)), dma((3,)), dma((3,)),
            pltpu.SemaphoreType.REGULAR, pltpu.SemaphoreType.REGULAR,
        ],
        compiler_params=pltpu.CompilerParams(
            collective_id=0, has_side_effects=True, vmem_limit_bytes=67043328
        ),
        name="panel_update",
    )(
        counts, col_index, barrier.reshape(-1, BW), border,
        inverse.reshape(Y, ZH, CORES * SHARE, PANEL), slab,
    )


def solution(mesh):
    return jax.shard_map(
        body,
        mesh=mesh,
        in_specs=(P("scen", "row", None), P("scen", None), P(), P(), P(), P("row", "scen")),
        out_specs=P("row", "scen"),
        check_vma=False,
    )
```
